32 devices in a mesh: dp: 16 (over z, y, x), mp: 2 (over core).
Axes of the slice: x: 2, y: 2, z: 4, core: 2. Of those that a mesh axis runs over, the one named last changes fastest.
Arguments:
- inputs: bfloat16 [32768, 4096], P('dp', 'mp'), may hold values from -6 to 6
- cotangents: bfloat16 [32768, 4096], P('dp', 'mp'), may hold values from -6 to 6
- loss_token_mask: int32 [32768], P('dp'), may hold values 0 or 1
- adapter_down_weight: bfloat16 [128, 4096], P(None, 'mp'), may hold values from -0.09375 to 0.09375
- adapter_up_weight: bfloat16 [4096, 128], P('mp'), may hold values from -0.5 to 0.5
- width_projection: bfloat16 [2, 4096, 256], P(None, 'mp'), may hold values from -0.09375 to 0.09375
- rank_projection: bfloat16 [2, 128, 16], replicated, may hold values from -0.5 to 0.5
- targets: float32 [64, 8192], P(None, ('dp', 'mp')), may hold values from -500 to 500
Outputs:
- scores: float32 [128, 64], P('dp')
The draws below stay inside these ranges and needn't reach their ends.
All inputs are finite; a program needn't handle non-finite values. No bound on the sum of `loss_token_mask` on one device may be relied on, other than what follows from the above.
Results may differ from the reference program's by a relative error of at most 0.0003.
Values sent between devices are 32-bit elements; how exact they have to be, the bound alone decides.
A program may use at most 64 MiB of HBM per device.

```python
import math
import jax
import jax.numpy as jnp
from jax import lax

MODEL_WIDTH = 4096
ADAPTER_RANK = 128
SEQ = 256
KP = 256
KQ = 16
NT = 64
FEAT = 8192
NCAND = 128
TOKENS = 32768


def draw_targets(key, part):
    first_matrix, second_matrix = jax.random.split(jax.random.fold_in(key, 17), 2)
    column_scale = jnp.exp(jax.random.uniform(second_matrix, (1, FEAT), jnp.float32, 0.0, math.log(10.0)))
    values = jnp.clip(jax.random.normal(first_matrix, (NT, FEAT), jnp.float32), -4.0, 4.0) * column_scale
    return values.astype(jnp.float32)


def touch_ends(values, key, least, high):
    place = [jax.random.randint(jax.random.fold_in(key, axis), (), 0, length) for axis, length in enumerate(values.shape)]
    main_axis = values.shape.index(max(values.shape))
    next_to = place[:main_axis] + [(place[main_axis] + 1) % values.shape[main_axis]] + place[main_axis + 1:]
    return values.at[tuple(place)].set(least).at[tuple(next_to)].set(high)


def block_scale(stream_key, extent, shards, least, top_value):
    gain = 1.0
    for position, parts in shards:
        heights = jax.random.uniform(jax.random.fold_in(jax.random.fold_in(stream_key, 6), position), (parts,), jnp.float32, least / len(shards), top_value / len(shards))
        gain = gain * jnp.repeat(jnp.exp(heights), extent[position] // parts).reshape((-1,) + (1,) * (len(extent) - 1 - position))
    return gain


def bell_draw(stream_key, shape, spread, bound, pieces=(), kind=jnp.bfloat16):
    drawn = spread * jax.random.normal(stream_key, shape, jnp.float32)
    if pieces:
        drawn = drawn * block_scale(stream_key, shape, pieces, -0.22, 0.18)
    return jnp.clip(drawn, -bound, bound).astype(kind)


def setup_inputs(seed: int = 0) -> dict:
    streams_of = jax.random.split(jax.random.key(seed), 9)
    return {
        "inputs": bell_draw(streams_of[0], (TOKENS, MODEL_WIDTH), 1.0, 6.0, ((0, 16), (1, 2))),
        "cotangents": bell_draw(streams_of[1], (TOKENS, MODEL_WIDTH), 1.0, 6.0, ((0, 16), (1, 2))),
        "loss_token_mask": touch_ends((jax.random.randint(streams_of[2], (TOKENS,), 0, 4) < 3).astype(jnp.int32), jax.random.fold_in(streams_of[2], 1), 0, 1),
        "adapter_down_weight": bell_draw(streams_of[3], (ADAPTER_RANK, MODEL_WIDTH), MODEL_WIDTH ** -0.5, 0.09375, ((1, 2),)),
        "adapter_up_weight": bell_draw(streams_of[4], (MODEL_WIDTH, ADAPTER_RANK), ADAPTER_RANK ** -0.5, 0.5, ((0, 2),)),
        "width_projection": bell_draw(streams_of[5], (2, MODEL_WIDTH, KP), MODEL_WIDTH ** -0.5, 0.09375, ((1, 2),)),
        "rank_projection": bell_draw(streams_of[6], (2, ADAPTER_RANK, KQ), ADAPTER_RANK ** -0.5, 0.5),
        "targets": draw_targets(jax.random.fold_in(streams_of[8], 71), 0),
    }


adapter_scale = 4.0
epsilon = 1e-06

def reference(inputs, cotangents, loss_token_mask, adapter_down_weight, adapter_up_weight, width_projection, rank_projection, targets):
    cols_first = rank_projection[0].astype(jnp.float32)
    cols_second = rank_projection[1].astype(jnp.float32)
    down_weight_wide = adapter_down_weight.astype(jnp.float32)
    up_weight_wide = adapter_up_weight.astype(jnp.float32)
    first_projection = width_projection[0].astype(jnp.float32)
    second_projection = width_projection[1].astype(jnp.float32)

    def one_sample(index):
        start = (index * SEQ).astype(jnp.int32)
        layer_activations = lax.dynamic_slice_in_dim(inputs, start, SEQ, 0)
        grads_out = lax.dynamic_slice_in_dim(cotangents, start, SEQ, 0)
        flags = lax.dynamic_slice_in_dim(loss_token_mask, start, SEQ, 0)
        masked_gradient = grads_out * flags.astype(jnp.bfloat16)[:, None]
        wide_activations = layer_activations.astype(jnp.float32)
        wide_masked = masked_gradient.astype(jnp.float32)
        down_rank_product = jnp.dot(wide_activations, down_weight_wide.T, precision=lax.Precision.HIGHEST)
        up_rank_product = jnp.dot(wide_masked, up_weight_wide, precision=lax.Precision.HIGHEST)
        projected_activations = jnp.dot(wide_activations, first_projection, precision=lax.Precision.HIGHEST)
        projected_masked_gradient = jnp.dot(wide_masked, second_projection, precision=lax.Precision.HIGHEST)
        compact_up_gradient = jnp.dot(up_rank_product, cols_first, precision=lax.Precision.HIGHEST)
        compact_down_gradient = jnp.dot(down_rank_product, cols_second, precision=lax.Precision.HIGHEST)
        first_matrix = adapter_scale * jnp.dot(projected_activations.T, compact_up_gradient, precision=lax.Precision.HIGHEST)
        second_matrix = adapter_scale * jnp.dot(projected_masked_gradient.T, compact_down_gradient, precision=lax.Precision.HIGHEST)
        return jnp.concatenate([first_matrix.reshape(-1), second_matrix.reshape(-1)])
    features = lax.map(one_sample, jnp.arange(NCAND, dtype=jnp.int32))
    inner = jnp.dot(features, targets.T, precision=lax.Precision.HIGHEST)
    sample_rms = jnp.sqrt(lax.optimization_barrier(jnp.mean(features * features, axis=1)) + epsilon)
    target_rms = jnp.sqrt(lax.optimization_barrier(jnp.mean(targets * targets, axis=1)) + epsilon)
    return inner / (math.sqrt(FEAT) * sample_rms[:, None] * target_rms[None, :])
```

```python
import functools
import math

import jax
import jax.numpy as jnp
from jax import lax
from jax.experimental import pallas as pl
from jax.experimental.pallas import tpu as pltpu
from jax.sharding import PartitionSpec as P

SEQ = 256
KP = 256
KQ = 16
FEAT = 8192
AHEAD = 2
LAG = 3

adapter_scale = 4.0
epsilon = 1e-06

f32 = jnp.float32
bf16 = jnp.bfloat16
NT = (((1,), (1,)), ((), ()))


def split(value):
    high = value.astype(bf16)
    low = (value - high.astype(f32)).astype(bf16)
    return high, low


def kernel(
    samples,
    x_hbm, g_hbm, mask_hbm, down_hbm, up_hbm, wp_hbm, rp_hbm, tgt_hbm, out_ref,
    xv, gv, dv, uv, wv, mv, rv, tv, lhs, ph, pw, cs, cr, tp, tt, ts, th, tl, fs, fr, ft, es, er,
    xsem, gsem, wsem, tsend, trecv, csend, crecv, fsend, frecv, esend, erecv,
):
    me = lax.axis_index("dp")
    core = lax.axis_index("mp")
    z = lax.div(me, 4)
    mine_p = lax.rem(me, 4)
    place = mine_p * 2 + core
    matrix = lax.div(z, 2)
    plane = lax.rem(z, 2)
    partner = me + 8 - 16 * matrix
    nt = tv.shape[0]
    mesh_ids = pl.DeviceIdType.MESH

    tgt_copy = pltpu.make_async_copy(tgt_hbm, tv, wsem.at[0])
    rp_copy = pltpu.make_async_copy(rp_hbm, rv, wsem.at[1])
    down_copy = pltpu.make_async_copy(down_hbm, dv, wsem.at[2])
    up_copy = pltpu.make_async_copy(up_hbm, uv, wsem.at[3])
    mask_copy = pltpu.make_async_copy(mask_hbm, mv, wsem.at[4])

    def wp_copy(j):
        return pltpu.make_async_copy(wp_hbm.at[j], wv.at[j], wsem.at[5 + j])

    def x_copy(n):
        rows = pl.ds(pl.multiple_of(n * SEQ, SEQ), SEQ)
        return pltpu.make_async_copy(x_hbm.at[rows], xv.at[n], xsem.at[n])

    def g_copy(n):
        rows = pl.ds(pl.multiple_of(n * SEQ, SEQ), SEQ)
        return pltpu.make_async_copy(g_hbm.at[rows], gv.at[n], gsem.at[n])

    tgt_copy.start()
    rp_copy.start()
    down_copy.start()
    up_copy.start()
    mask_copy.start()
    for j in range(2):
        wp_copy(j).start()
    for n in range(AHEAD):
        x_copy(n).start()
        g_copy(n).start()

    def flipped(mask):
        there = me
        for bit in range(3):
            if mask >> bit & 1:
                there = there + (1 << bit) * (1 - 2 * lax.rem(lax.div(me, 1 << bit), 2))
        return there

    peer = {"dp": me, "mp": 1 - core}
    barrier = pltpu.get_barrier_semaphore()

    def greet(device):
        pl.semaphore_signal(barrier, inc=1, device_id=device, device_id_type=mesh_ids)

    source_base = (2 * matrix + core) * 4
    greet(peer)
    for c in range(2):
        greet({"dp": partner, "mp": c})
    for p in range(4):
        for c in range(2):
            there = source_base + p
            known = (there == me)

            @pl.when(jnp.logical_not(known))
            def _():
                greet({"dp": there, "mp": c})

    tgt_copy.wait()
    turned = tv[...].T
    tp[:, 0:nt] = turned
    tp[:, nt : 2 * nt] = turned
    lane = lax.broadcasted_iota(jnp.int32, (KQ, 2 * nt), 1)
    for pair in range(KQ // 2):
        even = tp[pl.ds(2 * pair, KQ, stride=KQ), :]
        odd = tp[pl.ds(2 * pair + 1, KQ, stride=KQ), :]
        tt[:, pair * 2 * nt : (pair + 1) * 2 * nt] = jnp.where(lane < nt, even, odd)

    rp_copy.wait()
    down_copy.wait()
    first = jnp.dot(rv[1], dv[...], preferred_element_type=f32)
    high, low = split(first)
    lhs[0, KP : KP + KQ] = high
    lhs[0, KP + KQ : KP + 2 * KQ] = low
    up_copy.wait()
    second = lax.dot_general(rv[0], uv[...], NT, preferred_element_type=f32)
    high, low = split(second)
    lhs[1, KP : KP + KQ] = high
    lhs[1, KP + KQ : KP + 2 * KQ] = low
    for j in range(2):
        wp_copy(j).wait()
        lhs[j, 0:KP] = wv[j].T

    def t_copy(m):
        return pltpu.make_async_remote_copy(
            src_ref=tt, dst_ref=ts.at[place], send_sem=tsend.at[m], recv_sem=trecv.at[place],
            device_id={"dp": flipped(m), "mp": plane}, device_id_type=mesh_ids,
        )

    def t_arrival(i):
        return pltpu.make_async_remote_copy(
            src_ref=tt, dst_ref=ts.at[i], send_sem=tsend.at[0], recv_sem=trecv.at[i],
            device_id=peer, device_id_type=mesh_ids,
        )

    def c_copy(n):
        return pltpu.make_async_remote_copy(
            src_ref=cs.at[n], dst_ref=cr.at[n], send_sem=csend.at[n], recv_sem=crecv.at[n],
            device_id=peer, device_id_type=mesh_ids,
        )

    def f_near(n):
        return pltpu.make_async_remote_copy(
            src_ref=fs.at[n, matrix, 1 - core], dst_ref=fr.at[core, n],
            send_sem=fsend.at[2, n], recv_sem=frecv.at[core, n],
            device_id=peer, device_id_type=mesh_ids,
        )

    def f_far(n, h):
        return pltpu.make_async_remote_copy(
            src_ref=fs.at[n, 1 - matrix, h], dst_ref=fr.at[2 + core, n],
            send_sem=fsend.at[h, n], recv_sem=frecv.at[2 + core, n],
            device_id={"dp": partner, "mp": h}, device_id_type=mesh_ids,
        )

    def f_arrival(source, n):
        return pltpu.make_async_remote_copy(
            src_ref=fs.at[n, 0, 0], dst_ref=fr.at[source, n],
            send_sem=fsend.at[0, n], recv_sem=frecv.at[source, n],
            device_id=peer, device_id_type=mesh_ids,
        )

    def phase_one(n):
        for j, data in enumerate((xv, gv)):
            out = lax.dot_general(lhs[j], data[n], NT, preferred_element_type=f32)
            high, low = split(out[0:KP])
            ph[n, j] = high
            pw[n, j] = low
            cs[n, j * KQ : (j + 1) * KQ] = out[KP : KP + KQ] + out[KP + KQ : KP + 2 * KQ]

    def phase_two(n):
        flags = mv[n].astype(f32) * adapter_scale
        total = (cs[n] + cr[n]) * flags
        for j in range(2):
            high, low = split(total[(1 - j) * KQ : (2 - j) * KQ])
            stacked = jnp.concatenate([high, low], axis=0)
            out = lax.dot_general(stacked, ph[n, j], NT, preferred_element_type=f32)
            rest = lax.dot_general(high, pw[n, j], NT, preferred_element_type=f32)
            feature = out[0:KQ] + out[KQ : 2 * KQ] + rest
            for h in range(2):
                fs[n, j, h] = feature[:, h * 128 : (h + 1) * 128]

    def fetch(n):
        x_copy(n).wait()
        g_copy(n).wait()

        @pl.when(n + AHEAD < samples)
        def _():
            x_copy(n + AHEAD).start()
            g_copy(n + AHEAD).start()

    def send_features(n):
        for h in range(2):
            f_far(n, h).start()
        f_near(n).start()

    def only_one(n, carry):
        fetch(n)
        phase_one(n)
        return carry

    def both(n, carry):
        fetch(n)
        c_copy(n - LAG).wait_recv()
        phase_one(n)
        phase_two(n - LAG)
        c_copy(n).start()
        send_features(n - LAG)
        return carry

    def only_two(n, carry):
        c_copy(n).wait_recv()
        phase_two(n)
        send_features(n)
        return carry

    def start_c(n, carry):
        c_copy(n).start()
        return carry

    lax.fori_loop(0, LAG, only_one, 0)
    pl.semaphore_wait(barrier, 10)
    lax.fori_loop(0, LAG, start_c, 0)
    for m in range(7, 0, -1):
        t_copy(m).start()

    @pl.when(core != plane)
    def _():
        t_copy(0).start()

    @pl.when(core == plane)
    def _():
        ts[place] = tt[...]

    mask_copy.wait()
    lax.fori_loop(LAG, samples, both, 0)
    lax.fori_loop(samples - LAG, samples, only_two, 0)

    for i in range(8):
        @pl.when(jnp.logical_or(core != plane, place != i))
        def _():
            t_arrival(i).wait_recv()

    held = ts[...].reshape(8 * KQ, KQ * nt)
    t_high, t_low = split(held)
    th[0 : 8 * KQ] = t_high
    th[8 * KQ : 16 * KQ] = t_high
    tl[...] = t_low
    squares = jnp.sum((held * held).reshape(KQ, 8, KQ * nt), axis=0)
    folded = squares[:, 0 : 2 * nt]
    for piece in range(1, KQ // 2):
        folded = folded + squares[:, piece * 2 * nt : (piece + 1) * 2 * nt]
    left_lane = lax.broadcasted_iota(jnp.int32, (samples, 2 * nt), 1) < nt

    def score(side):
        if side == 0:
            total = fr[1 - core] + fs[:, matrix, core]
        else:
            total = fr[2] + fr[3]
        ft[side] = total.reshape(samples * KQ, 128)
        power = None
        even = None
        odd = None
        for step in range(4):
            rows = [ft[side, pl.ds(4 * step + r, samples, stride=KQ), :] for r in range(4)]
            for row in rows:
                power = row * row if power is None else power + row * row
            high, low = split(jnp.concatenate(rows, axis=0))
            cols = slice(step * 4 * nt, (step + 1) * 4 * nt)
            out = jnp.dot(jnp.concatenate([high, low], axis=1), th[:, cols], preferred_element_type=f32)
            out = out + jnp.dot(high, tl[:, cols], preferred_element_type=f32)
            first = out[0:samples, 0 : 2 * nt] + out[2 * samples : 3 * samples, 2 * nt : 4 * nt]
            second = out[samples : 2 * samples, 0 : 2 * nt] + out[3 * samples : 4 * samples, 2 * nt : 4 * nt]
            even = first if even is None else even + first
            odd = second if odd is None else odd + second
        inner = jnp.where(left_lane, even, odd)
        inner = inner + pltpu.roll(inner, nt, 1)
        power = power + pltpu.roll(power, nt, 1)
        es[side, 0:samples] = jnp.where(left_lane, inner, power)
        es[side, samples : samples + 8] = folded

    def e_near():
        return pltpu.make_async_remote_copy(
            src_ref=es.at[0], dst_ref=er.at[core], send_sem=esend.at[2], recv_sem=erecv.at[core],
            device_id=peer, device_id_type=mesh_ids,
        )

    def e_far(h):
        return pltpu.make_async_remote_copy(
            src_ref=es.at[1], dst_ref=er.at[2 + core], send_sem=esend.at[h], recv_sem=erecv.at[2 + core],
            device_id={"dp": partner, "mp": h}, device_id_type=mesh_ids,
        )

    def e_arrival(source):
        return pltpu.make_async_remote_copy(
            src_ref=es.at[0], dst_ref=er.at[source], send_sem=esend.at[0], recv_sem=erecv.at[source],
            device_id=peer, device_id_type=mesh_ids,
        )

    def near_arrived(n, carry):
        f_arrival(1 - core, n).wait_recv()
        return carry

    def far_arrived(n, carry):
        f_arrival(2, n).wait_recv()
        f_arrival(3, n).wait_recv()
        return carry

    def all_sent(n, carry):
        c_copy(n).wait_send()
        f_near(n).wait_send()
        for h in range(2):
            f_far(n, h).wait_send()
        return carry

    lax.fori_loop(0, samples, near_arrived, 0)
    score(0)
    e_near().start()
    er[core] = es[0]
    lax.fori_loop(0, samples, far_arrived, 0)
    score(1)
    for h in range(2):
        e_far(h).start()
    lax.fori_loop(0, samples, all_sent, 0)
    for m in range(1, 8):
        t_copy(m).wait_send()

    @pl.when(core != plane)
    def _():
        t_copy(0).wait_send()

    e_arrival(1 - core).wait_recv()
    for source in (2, 3):
        e_arrival(source).wait_recv()
    total = er[0] + er[1] + er[2] + er[3]
    target_squares = jnp.sum(total[samples : samples + 8], axis=0, keepdims=True)
    target_squares = target_squares[:, 0:nt] + target_squares[:, nt : 2 * nt]
    target_rms = jnp.sqrt(target_squares / FEAT + epsilon)
    sample_squares = jnp.sum(total[0:samples, nt : 2 * nt], axis=1, keepdims=True)
    sample_rms = jnp.sqrt(sample_squares / FEAT + epsilon)
    out_ref[...] = total[0:samples, 0:nt] / (math.sqrt(FEAT) * sample_rms * target_rms)
    e_near().wait_send()
    for h in range(2):
        e_far(h).wait_send()


def fused(inputs, cotangents, loss_token_mask, adapter_down_weight, adapter_up_weight,
          width_projection, rank_projection, targets):
    samples = inputs.shape[0] // SEQ
    width = inputs.shape[1]
    rank = adapter_down_weight.shape[0]
    nt = targets.shape[0]
    any_spec = pl.BlockSpec(memory_space=pl.ANY)
    vmem = pl.BlockSpec(memory_space=pltpu.VMEM)
    dma = pltpu.SemaphoreType.DMA
    return pl.pallas_call(
        functools.partial(kernel, samples),
        out_shape=pltpu.VMEM((samples, nt), f32),
        in_specs=[any_spec] * 8,
        out_specs=vmem,
        scratch_shapes=[
            pltpu.VMEM((samples, SEQ, width), bf16),
            pltpu.VMEM((samples, SEQ, width), bf16),
            pltpu.VMEM((rank, width), bf16),
            pltpu.VMEM((width, rank), bf16),
            pltpu.VMEM((2, width, KP), bf16),
            pltpu.VMEM((samples, 1, SEQ), jnp.int32),
            pltpu.VMEM((2, KQ, rank), bf16),
            pltpu.VMEM((nt, KQ * KQ), f32),
            pltpu.VMEM((2, KP + 2 * KQ, width), bf16),
            pltpu.VMEM((samples, 2, KP, SEQ), bf16),
            pltpu.VMEM((samples, 2, KP, SEQ), bf16),
            pltpu.VMEM((samples, 2 * KQ, SEQ), f32),
            pltpu.VMEM((samples, 2 * KQ, SEQ), f32),
            pltpu.VMEM((KQ * KQ, 2 * nt), f32),
            pltpu.VMEM((KQ, KQ * nt), f32),
            pltpu.VMEM((8, KQ, KQ * nt), f32),
            pltpu.VMEM((16 * KQ, KQ * nt), bf16),
            pltpu.VMEM((8 * KQ, KQ * nt), bf16),
            pltpu.VMEM((samples, 2, 2, KQ, 128), f32),
            pltpu.VMEM((4, samples, KQ, 128), f32),
            pltpu.VMEM((2, samples * KQ, 128), f32),
            pltpu.VMEM((2, samples + 8, 2 * nt), f32),
            pltpu.VMEM((4, samples + 8, 2 * nt), f32),
            dma((samples,)), dma((samples,)), dma((7,)),
            dma((8,)), dma((8,)),
            dma((samples,)), dma((samples,)),
            dma((3, samples)), dma((4, samples)),
            dma((3,)), dma((4,)),
        ],
        compiler_params=pltpu.CompilerParams(
            collective_id=0, has_side_effects=True, vmem_limit_bytes=52 << 20
        ),
        name="influence",
    )(inputs, cotangents, loss_token_mask.reshape(samples, 1, SEQ), adapter_down_weight,
      adapter_up_weight, width_projection, jnp.swapaxes(rank_projection, 1, 2), targets)


def general(inputs, cotangents, loss_token_mask, adapter_down_weight, adapter_up_weight,
            width_projection, rank_projection, targets):
    samples = inputs.shape[0] // SEQ
    masked_gradient = cotangents * loss_token_mask.astype(bf16)[:, None]
    cols_first = rank_projection[0].astype(f32)
    cols_second = rank_projection[1].astype(f32)
    down_partial = jnp.dot(inputs, adapter_down_weight.T, preferred_element_type=f32)
    up_partial = jnp.dot(masked_gradient, adapter_up_weight, preferred_element_type=f32)
    exact = lax.Precision.HIGHEST
    compact_up, compact_down = lax.psum(
        (jnp.dot(up_partial, cols_first, precision=exact), jnp.dot(down_partial, cols_second, precision=exact)), "mp"
    )
    projected_x = jnp.dot(inputs, width_projection[0], preferred_element_type=f32).reshape(samples, SEQ, KP)
    projected_g = jnp.dot(masked_gradient, width_projection[1], preferred_element_type=f32).reshape(samples, SEQ, KP)
    first = adapter_scale * jnp.einsum(
        "stk,stq->skq", projected_x, compact_up.reshape(samples, SEQ, KQ), precision=exact)
    second = adapter_scale * jnp.einsum(
        "stk,stq->skq", projected_g, compact_down.reshape(samples, SEQ, KQ), precision=exact)
    partial_value = jnp.concatenate([first.reshape(samples, -1), second.reshape(samples, -1)], axis=1)
    features = lax.psum(partial_value, "mp")
    every_target = lax.all_gather(targets, ("dp", "mp"), axis=1, tiled=True)
    inner = jnp.dot(features, every_target.T, precision=exact)
    sample_rms = jnp.sqrt(jnp.sum(features * features, axis=1) / FEAT + epsilon)
    target_rms = jnp.sqrt(jnp.sum(every_target * every_target, axis=1) / FEAT + epsilon)
    return inner / (math.sqrt(FEAT) * sample_rms[:, None] * target_rms[None, :])


def solution(mesh):
    n_dp, n_mp = mesh.shape["dp"], mesh.shape["mp"]
    fits = n_mp == 2 and n_dp * n_mp * KQ * KQ == FEAT

    def on_device(*args):
        eight = args[0].shape[0] == 8 * SEQ
        return fused(*args) if fits and eight else general(*args)

    in_specs = (
        P("dp", "mp"), P("dp", "mp"), P("dp"), P(None, "mp"), P("mp", None), P(None, "mp", None), P(),
        P(None, ("dp", "mp")),
    )
    return jax.shard_map(on_device, mesh=mesh, in_specs=in_specs, out_specs=P("dp", None), check_vma=False)
```

```python
import functools
import math

import jax
import jax.numpy as jnp
from jax import lax
from jax.experimental import pallas as pl
from jax.experimental.pallas import tpu as pltpu
from jax.sharding import PartitionSpec as P

SEQ = 256
KP = 256
KQ = 16
FEAT = 8192
LAG = 3
PASS = 6

adapter_scale = 4.0
epsilon = 1e-06

f32 = jnp.float32
bf16 = jnp.bfloat16
NT = (((1,), (1,)), ((), ()))


def split(value):
    high = value.astype(bf16)
    low = (value - high.astype(f32)).astype(bf16)
    return high, low


def kernel(
    samples,
    x_hbm, g_hbm, mask_hbm, down_hbm, up_hbm, wp_hbm, rp_hbm, tgt_hbm, out_ref,
    xv, gv, dv, uv, wv, mv, rv, tv, lhs, ph, pw, cs, cr, tp, tt, ts, th, tl, fs, fr, ft, es, er,
    xsem, gsem, wsem, tsend, trecv, csend, crecv, fsend, frecv, esend, erecv,
):
    me = lax.axis_index("dp")
    core = lax.axis_index("mp")
    z = lax.div(me, 4)
    mine_p = lax.rem(me, 4)
    y = lax.div(mine_p, 2)
    x = lax.rem(mine_p, 2)
    matrix = lax.div(z, 2)
    plane = lax.rem(z, 2)
    slot = plane * 4 + y * 2 + core
    partner = me + 1 - 2 * x
    beyond = me + 8 - 16 * matrix
    holder = core == matrix
    nt = tv.shape[0]
    mesh_ids = pl.DeviceIdType.MESH

    tgt_copy = pltpu.make_async_copy(tgt_hbm, tv, wsem.at[0])
    rp_copy = pltpu.make_async_copy(rp_hbm, rv, wsem.at[1])
    down_copy = pltpu.make_async_copy(down_hbm, dv, wsem.at[2])
    up_copy = pltpu.make_async_copy(up_hbm, uv, wsem.at[3])
    mask_copy = pltpu.make_async_copy(mask_hbm, mv, wsem.at[4])

    def wp_copy(j):
        return pltpu.make_async_copy(wp_hbm.at[j], wv.at[j], wsem.at[5 + j])

    def x_copy(n):
        rows = pl.ds(pl.multiple_of(n * SEQ, SEQ), SEQ)
        return pltpu.make_async_copy(x_hbm.at[rows], xv.at[n], xsem.at[n])

    def g_copy(n):
        rows = pl.ds(pl.multiple_of(n * SEQ, SEQ), SEQ)
        return pltpu.make_async_copy(g_hbm.at[rows], gv.at[n], gsem.at[n])

    tgt_copy.start()
    rp_copy.start()
    down_copy.start()
    up_copy.start()
    mask_copy.start()
    for j in range(2):
        wp_copy(j).start()
    x_copy(0).start()
    g_copy(0).start()

    peer = {"dp": me, "mp": 1 - core}

    def close(m):
        there = me
        if m % 2:
            there = there + 2 - 4 * y
        if m // 2:
            there = there + 4 - 8 * plane
        return there

    barrier = pltpu.get_barrier_semaphore()

    def greet(device):
        pl.semaphore_signal(barrier, inc=1, device_id=device, device_id_type=mesh_ids)

    greet(peer)
    for c in range(2):
        greet({"dp": partner, "mp": c})
    for m in range(1, 4):
        greet({"dp": close(m), "mp": core})

    @pl.when(holder)
    def _():
        for m in range(1, 4):
            greet({"dp": close(m), "mp": 1 - core})

    @pl.when(jnp.logical_not(holder))
    def _():
        for c in range(2):
            greet({"dp": beyond, "mp": c})

    tgt_copy.wait()
    turned = tv[...].T
    tp[:, 0:nt] = turned
    tp[:, nt : 2 * nt] = turned
    lane = lax.broadcasted_iota(jnp.int32, (KQ, 2 * nt), 1)
    for pair in range(KQ // 2):
        even = tp[pl.ds(2 * pair, KQ, stride=KQ), :]
        odd = tp[pl.ds(2 * pair + 1, KQ, stride=KQ), :]
        tt[:, pair * 2 * nt : (pair + 1) * 2 * nt] = jnp.where(lane < nt, even, odd)

    rp_copy.wait()
    down_copy.wait()
    first = jnp.dot(rv[1], dv[...], preferred_element_type=f32)
    high, low = split(first)
    lhs[0, KP : KP + KQ] = high
    lhs[0, KP + KQ : KP + 2 * KQ] = low
    up_copy.wait()
    for n in range(1, samples):
        x_copy(n).start()
        g_copy(n).start()
    second = lax.dot_general(rv[0], uv[...], NT, preferred_element_type=f32)
    high, low = split(second)
    lhs[1, KP : KP + KQ] = high
    lhs[1, KP + KQ : KP + 2 * KQ] = low
    for j in range(2):
        wp_copy(j).wait()
        flat = wv[j].T
        for p in range(8):
            start = p % 2 * 128 + p // 2 * 32
            lhs[j, start : start + 32] = flat[p * 32 : (p + 1) * 32]

    def t_copy(way):
        if way < 3:
            there = {"dp": close(way + 1), "mp": matrix}
        elif way == 3:
            there = {"dp": beyond, "mp": matrix}
        else:
            there = peer
        return pltpu.make_async_remote_copy(
            src_ref=tt, dst_ref=ts.at[slot], send_sem=tsend.at[way], recv_sem=trecv.at[slot],
            device_id=there, device_id_type=mesh_ids,
        )

    def t_pass(c, m):
        held = plane * 4 + y * 2 + c
        return pltpu.make_async_remote_copy(
            src_ref=ts.at[held], dst_ref=ts.at[held], send_sem=tsend.at[4 + c * 3 + m], recv_sem=trecv.at[held],
            device_id={"dp": close(m), "mp": core}, device_id_type=mesh_ids,
        )

    def t_arrival(i):
        return pltpu.make_async_remote_copy(
            src_ref=tt, dst_ref=ts.at[i], send_sem=tsend.at[0], recv_sem=trecv.at[i],
            device_id=peer, device_id_type=mesh_ids,
        )

    def c_copy(n):
        return pltpu.make_async_remote_copy(
            src_ref=cs.at[n], dst_ref=cr.at[n], send_sem=csend.at[n], recv_sem=crecv.at[n],
            device_id=peer, device_id_type=mesh_ids,
        )

    def f_near(n):
        return pltpu.make_async_remote_copy(
            src_ref=fs.at[n, 1 - core, x], dst_ref=fr.at[core, n],
            send_sem=fsend.at[2, n], recv_sem=frecv.at[core, n],
            device_id=peer, device_id_type=mesh_ids,
        )

    def f_far(n, h):
        return pltpu.make_async_remote_copy(
            src_ref=fs.at[n, h, 1 - x], dst_ref=fr.at[2 + core, n],
            send_sem=fsend.at[h, n], recv_sem=frecv.at[2 + core, n],
            device_id={"dp": partner, "mp": h}, device_id_type=mesh_ids,
        )

    def f_arrival(source, n):
        return pltpu.make_async_remote_copy(
            src_ref=fs.at[n, 0, 0], dst_ref=fr.at[source, n],
            send_sem=fsend.at[0, n], recv_sem=frecv.at[source, n],
            device_id=peer, device_id_type=mesh_ids,
        )

    def phase_one(n):
        for j, data in enumerate((xv, gv)):
            out = lax.dot_general(lhs[j], data[n], NT, preferred_element_type=f32)
            high, low = split(out[0:KP])
            ph[n, j] = high
            pw[n, j] = low
            cs[n, j * KQ : (j + 1) * KQ] = out[KP : KP + KQ] + out[KP + KQ : KP + 2 * KQ]

    def phase_two(n):
        flags = mv[n].astype(f32) * adapter_scale
        total = (cs[n] + cr[n]) * flags
        for j in range(2):
            high, low = split(total[(1 - j) * KQ : (2 - j) * KQ])
            stacked = jnp.concatenate([high, low], axis=0)
            out = lax.dot_general(stacked, ph[n, j], NT, preferred_element_type=f32)
            rest = lax.dot_general(high, pw[n, j], NT, preferred_element_type=f32)
            feature = out[0:KQ] + out[KQ : 2 * KQ] + rest
            for h in range(2):
                fs[n, j, h] = feature[:, h * 128 : (h + 1) * 128]

    def fetch(n):
        x_copy(n).wait()
        g_copy(n).wait()

    def send_features(n):
        for h in range(2):
            f_far(n, h).start()
        f_near(n).start()

    def only_one(n, carry):
        fetch(n)
        phase_one(n)
        return carry

    def both(n, carry):
        fetch(n)
        c_copy(n - LAG).wait_recv()
        phase_one(n)
        phase_two(n - LAG)
        c_copy(n).start()
        send_features(n - LAG)
        return carry

    def only_two(n, carry):
        c_copy(n).wait_recv()
        phase_two(n)
        send_features(n)
        return carry

    def start_c(n, carry):
        c_copy(n).start()
        return carry

    lax.fori_loop(0, LAG, only_one, 0)
    pl.semaphore_wait(barrier, jnp.where(holder, 7, 10))
    lax.fori_loop(0, LAG, start_c, 0)
    for way in (3, 0, 1, 2):
        t_copy(way).start()

    @pl.when(jnp.logical_not(holder))
    def _():
        t_copy(4).start()

    @pl.when(holder)
    def _():
        ts[slot] = tt[...]

    mask_copy.wait()
    lax.fori_loop(LAG, PASS, both, 0)

    @pl.when(jnp.logical_not(holder))
    def _():
        for c in range(2):
            t_arrival(plane * 4 + y * 2 + c).wait_recv()
            for m in range(1, 4):
                t_pass(c, m).start()

    lax.fori_loop(PASS, samples, both, 0)
    lax.fori_loop(samples - LAG, samples, only_two, 0)

    def take(line):
        total = None
        for p in range(2):
            start = pl.multiple_of(p * 4 + line * 2, 2)
            held = ts[pl.ds(start, 2)].reshape(2 * KQ, KQ * nt)
            t_high, t_low = split(held)
            row = pl.multiple_of(start * KQ, 2 * KQ)
            th[pl.ds(row, 2 * KQ)] = t_high
            th[pl.ds(row + 8 * KQ, 2 * KQ)] = t_high
            tl[pl.ds(row, 2 * KQ)] = t_low
            part = jnp.sum((held * held).reshape(4, 8, KQ * nt), axis=0)
            total = part if total is None else total + part
        folded = total[:, 0 : 2 * nt]
        for piece in range(1, KQ // 2):
            folded = folded + total[:, piece * 2 * nt : (piece + 1) * 2 * nt]
        return folded

    @pl.when(holder)
    def _():
        t_arrival(plane * 4 + y * 2 + 1 - core).wait_recv()

    for m in range(1, 4):
        row = y + (1 - 2 * y) * (m % 2)
        side = plane + (1 - 2 * plane) * (m // 2)
        for c in range(2):
            t_arrival(side * 4 + row * 2 + c).wait_recv()
    folded = take(0) + take(1)
    left_lane = lax.broadcasted_iota(jnp.int32, (samples, 2 * nt), 1) < nt

    def score(side):
        if side == 0:
            total = fr[1 - core] + fs[:, core, x]
        else:
            total = fr[2] + fr[3]
        ft[side] = total.reshape(samples * KQ, 128)
        power = None
        even = None
        odd = None
        for step in range(4):
            rows = [ft[side, pl.ds(4 * step + r, samples, stride=KQ), :] for r in range(4)]
            for row in rows:
                power = row * row if power is None else power + row * row
            high, low = split(jnp.concatenate(rows, axis=0))
            cols = slice(step * 4 * nt, (step + 1) * 4 * nt)
            out = jnp.dot(jnp.concatenate([high, low], axis=1), th[:, cols], preferred_element_type=f32)
            out = out + jnp.dot(high, tl[:, cols], preferred_element_type=f32)
            first = out[0:samples, 0 : 2 * nt] + out[2 * samples : 3 * samples, 2 * nt : 4 * nt]
            second = out[samples : 2 * samples, 0 : 2 * nt] + out[3 * samples : 4 * samples, 2 * nt : 4 * nt]
            even = first if even is None else even + first
            odd = second if odd is None else odd + second
        inner = jnp.where(left_lane, even, odd)
        inner = inner + pltpu.roll(inner, nt, 1)
        power = power + pltpu.roll(power, nt, 1)
        es[side, 0:samples] = jnp.where(left_lane, inner, power)
        es[side, samples : samples + 8] = folded

    def e_near():
        return pltpu.make_async_remote_copy(
            src_ref=es.at[0], dst_ref=er.at[core], send_sem=esend.at[2], recv_sem=erecv.at[core],
            device_id=peer, device_id_type=mesh_ids,
        )

    def e_far(h):
        return pltpu.make_async_remote_copy(
            src_ref=es.at[1], dst_ref=er.at[2 + core], send_sem=esend.at[h], recv_sem=erecv.at[2 + core],
            device_id={"dp": partner, "mp": h}, device_id_type=mesh_ids,
        )

    def e_arrival(source):
        return pltpu.make_async_remote_copy(
            src_ref=es.at[0], dst_ref=er.at[source], send_sem=esend.at[0], recv_sem=erecv.at[source],
            device_id=peer, device_id_type=mesh_ids,
        )

    def near_arrived(n, carry):
        f_arrival(1 - core, n).wait_recv()
        return carry

    def far_arrived(n, carry):
        f_arrival(2, n).wait_recv()
        f_arrival(3, n).wait_recv()
        return carry

    def all_sent(n, carry):
        c_copy(n).wait_send()
        f_near(n).wait_send()
        for h in range(2):
            f_far(n, h).wait_send()
        return carry

    lax.fori_loop(0, samples, near_arrived, 0)
    score(0)
    e_near().start()
    er[core] = es[0]
    lax.fori_loop(0, samples, far_arrived, 0)
    score(1)
    for h in range(2):
        e_far(h).start()
    lax.fori_loop(0, samples, all_sent, 0)
    for way in range(4):
        t_copy(way).wait_send()

    @pl.when(jnp.logical_not(holder))
    def _():
        t_copy(4).wait_send()

    @pl.when(jnp.logical_not(holder))
    def _():
        for c in range(2):
            for m in range(1, 4):
                t_pass(c, m).wait_send()

    e_arrival(1 - core).wait_recv()
    for source in (2, 3):
        e_arrival(source).wait_recv()
    total = er[0] + er[1] + er[2] + er[3]
    target_squares = jnp.sum(total[samples : samples + 8], axis=0, keepdims=True)
    target_squares = target_squares[:, 0:nt] + target_squares[:, nt : 2 * nt]
    target_rms = jnp.sqrt(target_squares / FEAT + epsilon)
    sample_squares = jnp.sum(total[0:samples, nt : 2 * nt], axis=1, keepdims=True)
    sample_rms = jnp.sqrt(sample_squares / FEAT + epsilon)
    out_ref[...] = total[0:samples, 0:nt] / (math.sqrt(FEAT) * sample_rms * target_rms)
    e_near().wait_send()
    for h in range(2):
        e_far(h).wait_send()


def fused(inputs, cotangents, loss_token_mask, adapter_down_weight, adapter_up_weight,
          width_projection, rank_projection, targets):
    samples = inputs.shape[0] // SEQ
    width = inputs.shape[1]
    rank = adapter_down_weight.shape[0]
    nt = targets.shape[0]
    any_spec = pl.BlockSpec(memory_space=pltpu.HBM)
    vmem = pl.BlockSpec(memory_space=pltpu.VMEM)
    dma = pltpu.SemaphoreType.DMA
    return pl.pallas_call(
        functools.partial(kernel, samples),
        out_shape=pltpu.VMEM((samples, nt), f32),
        in_specs=[any_spec] * 8,
        out_specs=vmem,
        scratch_shapes=[
            pltpu.VMEM((samples, SEQ, width), bf16),
            pltpu.VMEM((samples, SEQ, width), bf16),
            pltpu.VMEM((rank, width), bf16),
            pltpu.VMEM((width, rank), bf16),
            pltpu.VMEM((2, width, KP), bf16),
            pltpu.VMEM((samples, 1, SEQ), jnp.int32),
            pltpu.VMEM((2, KQ, rank), bf16),
            pltpu.VMEM((nt, KQ * KQ), f32),
            pltpu.VMEM((2, KP + 2 * KQ, width), bf16),
            pltpu.VMEM((samples, 2, KP, SEQ), bf16),
            pltpu.VMEM((samples, 2, KP, SEQ), bf16),
            pltpu.VMEM((samples, 2 * KQ, SEQ), f32),
            pltpu.VMEM((samples, 2 * KQ, SEQ), f32),
            pltpu.VMEM((KQ * KQ, 2 * nt), f32),
            pltpu.VMEM((KQ, KQ * nt), f32),
            pltpu.VMEM((8, KQ, KQ * nt), f32),
            pltpu.VMEM((16 * KQ, KQ * nt), bf16),
            pltpu.VMEM((8 * KQ, KQ * nt), bf16),
            pltpu.VMEM((samples, 2, 2, KQ, 128), f32),
            pltpu.VMEM((4, samples, KQ, 128), f32),
            pltpu.VMEM((2, samples * KQ, 128), f32),
            pltpu.VMEM((2, samples + 8, 2 * nt), f32),
            pltpu.VMEM((4, samples + 8, 2 * nt), f32),
            dma((samples,)), dma((samples,)), dma((7,)),
            dma((11,)), dma((8,)),
            dma((samples,)), dma((samples,)),
            dma((3, samples)), dma((4, samples)),
            dma((3,)), dma((4,)),
        ],
        compiler_params=pltpu.CompilerParams(
            collective_id=0, has_side_effects=True, vmem_limit_bytes=60 << 20
        ),
        name="influence",
    )(inputs, cotangents, loss_token_mask.reshape(samples, 1, SEQ), adapter_down_weight,
      adapter_up_weight, width_projection, jnp.swapaxes(rank_projection, 1, 2), targets)


def general(inputs, cotangents, loss_token_mask, adapter_down_weight, adapter_up_weight,
            width_projection, rank_projection, targets):
    samples = inputs.shape[0] // SEQ
    masked_gradient = cotangents * loss_token_mask.astype(bf16)[:, None]
    cols_first = rank_projection[0].astype(f32)
    cols_second = rank_projection[1].astype(f32)
    down_partial = jnp.dot(inputs, adapter_down_weight.T, preferred_element_type=f32)
    up_partial = jnp.dot(masked_gradient, adapter_up_weight, preferred_element_type=f32)
    exact = lax.Precision.HIGHEST
    compact_up, compact_down = lax.psum(
        (jnp.dot(up_partial, cols_first, precision=exact), jnp.dot(down_partial, cols_second, precision=exact)), "mp"
    )
    projected_x = jnp.dot(inputs, width_projection[0], preferred_element_type=f32).reshape(samples, SEQ, KP)
    projected_g = jnp.dot(masked_gradient, width_projection[1], preferred_element_type=f32).reshape(samples, SEQ, KP)
    first = adapter_scale * jnp.einsum(
        "stk,stq->skq", projected_x, compact_up.reshape(samples, SEQ, KQ), precision=exact)
    second = adapter_scale * jnp.einsum(
        "stk,stq->skq", projected_g, compact_down.reshape(samples, SEQ, KQ), precision=exact)
    partial_value = jnp.concatenate([first.reshape(samples, -1), second.reshape(samples, -1)], axis=1)
    features = lax.psum(partial_value, "mp")
    every_target = lax.all_gather(targets, ("dp", "mp"), axis=1, tiled=True)
    inner = jnp.dot(features, every_target.T, precision=exact)
    sample_rms = jnp.sqrt(jnp.sum(features * features, axis=1) / FEAT + epsilon)
    target_rms = jnp.sqrt(jnp.sum(every_target * every_target, axis=1) / FEAT + epsilon)
    return inner / (math.sqrt(FEAT) * sample_rms[:, None] * target_rms[None, :])


def solution(mesh):
    n_dp, n_mp = mesh.shape["dp"], mesh.shape["mp"]
    fits = n_mp == 2 and n_dp * n_mp * KQ * KQ == FEAT

    def on_device(*args):
        eight = args[0].shape[0] == 8 * SEQ
        return fused(*args) if fits and eight else general(*args)

    in_specs = (
        P("dp", "mp"), P("dp", "mp"), P("dp"), P(None, "mp"), P("mp", None), P(None, "mp", None), P(),
        P(None, ("dp", "mp")),
    )
    return jax.shard_map(on_device, mesh=mesh, in_specs=in_specs, out_specs=P("dp", None), check_vma=False)
```

```python
import functools
import math

import jax
import jax.numpy as jnp
from jax import lax
from jax.experimental import pallas as pl
from jax.experimental.pallas import tpu as pltpu
from jax.sharding import PartitionSpec as P

SEQ = 256
KP = 256
KQ = 16
FEAT = 8192
LAG = 3
PASS = 7
EARLY = 2
NEAR = 3

adapter_scale = 4.0
epsilon = 1e-06

f32 = jnp.float32
bf16 = jnp.bfloat16
NT = (((1,), (1,)), ((), ()))


def split(value):
    high = value.astype(bf16)
    low = (value - high.astype(f32)).astype(bf16)
    return high, low


def kernel(
    samples,
    x_hbm, g_hbm, mask_hbm, down_hbm, up_hbm, wp_hbm, rp_hbm, tgt_hbm, out_ref,
    xv, gv, dv, uv, wv, mv, rv, tv, lhs, ph, pw, cs, cr, tp, tt, ts, th, tl, fs, fr, ft, es, er,
    xsem, gsem, wsem, tsend, trecv, csend, crecv, fsend, frecv, esend, erecv,
):
    me = lax.axis_index("dp")
    core = lax.axis_index("mp")
    z = lax.div(me, 4)
    mine_p = lax.rem(me, 4)
    y = lax.div(mine_p, 2)
    x = lax.rem(mine_p, 2)
    matrix = lax.div(z, 2)
    plane = lax.rem(z, 2)
    slot = plane * 4 + y * 2 + core
    partner = me + 1 - 2 * x
    beyond = me + 8 - 16 * matrix
    holder = core == matrix
    nt = tv.shape[0]
    mesh_ids = pl.DeviceIdType.MESH

    tgt_copy = pltpu.make_async_copy(tgt_hbm, tv, wsem.at[0])
    rp_copy = pltpu.make_async_copy(rp_hbm, rv, wsem.at[1])
    down_copy = pltpu.make_async_copy(down_hbm, dv, wsem.at[2])
    up_copy = pltpu.make_async_copy(up_hbm, uv, wsem.at[3])
    mask_copy = pltpu.make_async_copy(mask_hbm, mv, wsem.at[4])

    def wp_copy(j):
        return pltpu.make_async_copy(wp_hbm.at[j], wv.at[j], wsem.at[5 + j])

    def x_copy(n):
        rows = pl.ds(pl.multiple_of(n * SEQ, SEQ), SEQ)
        return pltpu.make_async_copy(x_hbm.at[rows], xv.at[n], xsem.at[n])

    def g_copy(n):
        rows = pl.ds(pl.multiple_of(n * SEQ, SEQ), SEQ)
        return pltpu.make_async_copy(g_hbm.at[rows], gv.at[n], gsem.at[n])

    tgt_copy.start()
    rp_copy.start()
    down_copy.start()
    up_copy.start()
    mask_copy.start()
    for j in range(2):
        wp_copy(j).start()
    for n in range(samples):
        x_copy(n).start(priority=1)
        g_copy(n).start(priority=1)

    peer = {"dp": me, "mp": 1 - core}

    def close(m):
        there = me
        if m % 2:
            there = there + 2 - 4 * y
        if m // 2:
            there = there + 4 - 8 * plane
        return there

    barrier = pltpu.get_barrier_semaphore()

    def greet(device):
        pl.semaphore_signal(barrier, inc=1, device_id=device, device_id_type=mesh_ids)

    greet(peer)
    for c in range(2):
        greet({"dp": partner, "mp": c})
    for m in range(1, 4):
        greet({"dp": close(m), "mp": core})

    @pl.when(holder)
    def _():
        for m in range(1, 4):
            greet({"dp": close(m), "mp": 1 - core})

    @pl.when(jnp.logical_not(holder))
    def _():
        for c in range(2):
            greet({"dp": beyond, "mp": c})

    tgt_copy.wait()
    turned = tv[...].T
    tp[:, 0:nt] = turned
    tp[:, nt : 2 * nt] = turned
    lane = lax.broadcasted_iota(jnp.int32, (KQ, 2 * nt), 1)
    for pair in range(KQ // 2):
        even = tp[pl.ds(2 * pair, KQ, stride=KQ), :]
        odd = tp[pl.ds(2 * pair + 1, KQ, stride=KQ), :]
        tt[:, pair * 2 * nt : (pair + 1) * 2 * nt] = jnp.where(lane < nt, even, odd)

    rp_copy.wait()
    down_copy.wait()
    first = jnp.dot(rv[1], dv[...], preferred_element_type=f32)
    high, low = split(first)
    lhs[0, KP : KP + KQ] = high
    lhs[0, KP + KQ : KP + 2 * KQ] = low
    up_copy.wait()
    second = lax.dot_general(rv[0], uv[...], NT, preferred_element_type=f32)
    high, low = split(second)
    lhs[1, KP : KP + KQ] = high
    lhs[1, KP + KQ : KP + 2 * KQ] = low
    for j in range(2):
        wp_copy(j).wait()
        flat = wv[j].T
        for p in range(8):
            start = p % 2 * 128 + p // 2 * 32
            lhs[j, start : start + 32] = flat[p * 32 : (p + 1) * 32]

    def t_copy(way):
        if way < 3:
            there = {"dp": close(way + 1), "mp": matrix}
        elif way == 3:
            there = {"dp": beyond, "mp": matrix}
        else:
            there = peer
        return pltpu.make_async_remote_copy(
            src_ref=tt, dst_ref=ts.at[slot], send_sem=tsend.at[way], recv_sem=trecv.at[slot],
            device_id=there, device_id_type=mesh_ids,
        )

    def t_pass(c, m):
        held = plane * 4 + y * 2 + c
        return pltpu.make_async_remote_copy(
            src_ref=ts.at[held], dst_ref=ts.at[held], send_sem=tsend.at[4 + c * 3 + m], recv_sem=trecv.at[held],
            device_id={"dp": close(m), "mp": core}, device_id_type=mesh_ids,
        )

    def t_arrival(i):
        return pltpu.make_async_remote_copy(
            src_ref=tt, dst_ref=ts.at[i], send_sem=tsend.at[0], recv_sem=trecv.at[i],
            device_id=peer, device_id_type=mesh_ids,
        )

    def c_copy(n):
        return pltpu.make_async_remote_copy(
            src_ref=cs.at[n], dst_ref=cr.at[n], send_sem=csend.at[n], recv_sem=crecv.at[n],
            device_id=peer, device_id_type=mesh_ids,
        )

    def f_near(n):
        return pltpu.make_async_remote_copy(
            src_ref=fs.at[n, 1 - core, x], dst_ref=fr.at[core, n],
            send_sem=fsend.at[2, n], recv_sem=frecv.at[core, n],
            device_id=peer, device_id_type=mesh_ids,
        )

    def f_far(n, h):
        return pltpu.make_async_remote_copy(
            src_ref=fs.at[n, h, 1 - x], dst_ref=fr.at[2 + core, n],
            send_sem=fsend.at[h, n], recv_sem=frecv.at[2 + core, n],
            device_id={"dp": partner, "mp": h}, device_id_type=mesh_ids,
        )

    def f_arrival(source, n):
        return pltpu.make_async_remote_copy(
            src_ref=fs.at[n, 0, 0], dst_ref=fr.at[source, n],
            send_sem=fsend.at[0, n], recv_sem=frecv.at[source, n],
            device_id=peer, device_id_type=mesh_ids,
        )

    def phase_one(n):
        for j, data in enumerate((xv, gv)):
            out = lax.dot_general(lhs[j], data[n], NT, preferred_element_type=f32)
            high, low = split(out[0:KP])
            ph[n, j] = high
            pw[n, j] = low
            cs[n, j * KQ : (j + 1) * KQ] = out[KP : KP + KQ] + out[KP + KQ : KP + 2 * KQ]

    def phase_two(n):
        flags = mv[n].astype(f32) * adapter_scale
        total = (cs[n] + cr[n]) * flags
        for j in range(2):
            high, low = split(total[(1 - j) * KQ : (2 - j) * KQ])
            stacked = jnp.concatenate([high, low], axis=0)
            out = lax.dot_general(stacked, ph[n, j], NT, preferred_element_type=f32)
            rest = lax.dot_general(high, pw[n, j], NT, preferred_element_type=f32)
            feature = out[0:KQ] + out[KQ : 2 * KQ] + rest
            for h in range(2):
                fs[n, j, h] = feature[:, h * 128 : (h + 1) * 128]

    def fetch(n):
        x_copy(n).wait()
        g_copy(n).wait()

    def send_features(n):
        for h in range(2):
            f_far(n, h).start()
        f_near(n).start()

    def only_one(n, carry):
        fetch(n)
        phase_one(n)
        return carry

    def both(n, carry):
        fetch(n)
        c_copy(n - LAG).wait_recv()
        phase_one(n)
        phase_two(n - LAG)
        c_copy(n).start()
        send_features(n - LAG)
        return carry

    def only_two(n, carry):
        c_copy(n).wait_recv()
        phase_two(n)
        send_features(n)
        return carry

    def start_c(n, carry):
        c_copy(n).start()
        return carry

    lax.fori_loop(0, EARLY, only_one, 0)
    pl.semaphore_wait(barrier, jnp.where(holder, 7, 10))
    lax.fori_loop(0, EARLY, start_c, 0)
    t_copy(3).start()

    @pl.when(jnp.logical_not(holder))
    def _():
        t_copy(4).start()

    @pl.when(holder)
    def _():
        ts[slot] = tt[...]

    def one_more(n, carry):
        only_one(n, carry)
        c_copy(n).start()
        return carry

    lax.fori_loop(EARLY, LAG, one_more, 0)
    mask_copy.wait()
    for way in range(3):
        t_copy(way).start()
    lax.fori_loop(NEAR, PASS, both, 0)

    @pl.when(jnp.logical_not(holder))
    def _():
        for c in range(2):
            t_arrival(plane * 4 + y * 2 + c).wait_recv()
            for m in range(1, 4):
                t_pass(c, m).start()

    lax.fori_loop(PASS, samples, both, 0)
    lax.fori_loop(samples - LAG, samples, only_two, 0)

    def take(line):
        total = None
        for p in range(2):
            start = pl.multiple_of(p * 4 + line * 2, 2)
            held = ts[pl.ds(start, 2)].reshape(2 * KQ, KQ * nt)
            t_high, t_low = split(held)
            row = pl.multiple_of(start * KQ, 2 * KQ)
            th[pl.ds(row, 2 * KQ)] = t_high
            th[pl.ds(row + 8 * KQ, 2 * KQ)] = t_high
            tl[pl.ds(row, 2 * KQ)] = t_low
            part = jnp.sum((held * held).reshape(4, 8, KQ * nt), axis=0)
            total = part if total is None else total + part
        folded = total[:, 0 : 2 * nt]
        for piece in range(1, KQ // 2):
            folded = folded + total[:, piece * 2 * nt : (piece + 1) * 2 * nt]
        return folded

    @pl.when(holder)
    def _():
        t_arrival(plane * 4 + y * 2 + 1 - core).wait_recv()

    for m in range(1, 4):
        row = y + (1 - 2 * y) * (m % 2)
        side = plane + (1 - 2 * plane) * (m // 2)
        for c in range(2):
            t_arrival(side * 4 + row * 2 + c).wait_recv()
    folded = take(0) + take(1)
    left_lane = lax.broadcasted_iota(jnp.int32, (samples, 2 * nt), 1) < nt

    def score(side):
        if side == 0:
            total = fr[1 - core] + fs[:, core, x]
        else:
            total = fr[2] + fr[3]
        ft[side] = total.reshape(samples * KQ, 128)
        power = None
        even = None
        odd = None
        for step in range(4):
            rows = [ft[side, pl.ds(4 * step + r, samples, stride=KQ), :] for r in range(4)]
            for row in rows:
                power = row * row if power is None else power + row * row
            high, low = split(jnp.concatenate(rows, axis=0))
            cols = slice(step * 4 * nt, (step + 1) * 4 * nt)
            out = jnp.dot(jnp.concatenate([high, low], axis=1), th[:, cols], preferred_element_type=f32)
            out = out + jnp.dot(high, tl[:, cols], preferred_element_type=f32)
            first = out[0:samples, 0 : 2 * nt] + out[2 * samples : 3 * samples, 2 * nt : 4 * nt]
            second = out[samples : 2 * samples, 0 : 2 * nt] + out[3 * samples : 4 * samples, 2 * nt : 4 * nt]
            even = first if even is None else even + first
            odd = second if odd is None else odd + second
        inner = jnp.where(left_lane, even, odd)
        inner = inner + pltpu.roll(inner, nt, 1)
        power = power + pltpu.roll(power, nt, 1)
        es[side, 0:samples] = jnp.where(left_lane, inner, power)
        es[side, samples : samples + 8] = folded

    def e_near():
        return pltpu.make_async_remote_copy(
            src_ref=es.at[0], dst_ref=er.at[core], send_sem=esend.at[2], recv_sem=erecv.at[core],
            device_id=peer, device_id_type=mesh_ids,
        )

    def e_far(h):
        return pltpu.make_async_remote_copy(
            src_ref=es.at[1], dst_ref=er.at[2 + core], send_sem=esend.at[h], recv_sem=erecv.at[2 + core],
            device_id={"dp": partner, "mp": h}, device_id_type=mesh_ids,
        )

    def e_arrival(source):
        return pltpu.make_async_remote_copy(
            src_ref=es.at[0], dst_ref=er.at[source], send_sem=esend.at[0], recv_sem=erecv.at[source],
            device_id=peer, device_id_type=mesh_ids,
        )

    def near_arrived(n, carry):
        f_arrival(1 - core, n).wait_recv()
        return carry

    def far_arrived(n, carry):
        f_arrival(2, n).wait_recv()
        f_arrival(3, n).wait_recv()
        return carry

    def all_sent(n, carry):
        c_copy(n).wait_send()
        f_near(n).wait_send()
        for h in range(2):
            f_far(n, h).wait_send()
        return carry

    lax.fori_loop(0, samples, near_arrived, 0)
    score(0)
    e_near().start()
    er[core] = es[0]
    lax.fori_loop(0, samples, far_arrived, 0)
    score(1)
    for h in range(2):
        e_far(h).start()
    lax.fori_loop(0, samples, all_sent, 0)
    for way in range(4):
        t_copy(way).wait_send()

    @pl.when(jnp.logical_not(holder))
    def _():
        t_copy(4).wait_send()

    @pl.when(jnp.logical_not(holder))
    def _():
        for c in range(2):
            for m in range(1, 4):
                t_pass(c, m).wait_send()

    e_arrival(1 - core).wait_recv()
    for source in (2, 3):
        e_arrival(source).wait_recv()
    total = er[0] + er[1] + er[2] + er[3]
    target_squares = jnp.sum(total[samples : samples + 8], axis=0, keepdims=True)
    target_squares = target_squares[:, 0:nt] + target_squares[:, nt : 2 * nt]
    target_rms = jnp.sqrt(target_squares / FEAT + epsilon)
    sample_squares = jnp.sum(total[0:samples, nt : 2 * nt], axis=1, keepdims=True)
    sample_rms = jnp.sqrt(sample_squares / FEAT + epsilon)
    out_ref[...] = total[0:samples, 0:nt] / (math.sqrt(FEAT) * sample_rms * target_rms)
    e_near().wait_send()
    for h in range(2):
        e_far(h).wait_send()


def fused(inputs, cotangents, loss_token_mask, adapter_down_weight, adapter_up_weight,
          width_projection, rank_projection, targets):
    samples = inputs.shape[0] // SEQ
    width = inputs.shape[1]
    rank = adapter_down_weight.shape[0]
    nt = targets.shape[0]
    any_spec = pl.BlockSpec(memory_space=pltpu.HBM)
    vmem = pl.BlockSpec(memory_space=pltpu.VMEM)
    dma = pltpu.SemaphoreType.DMA
    return pl.pallas_call(
        functools.partial(kernel, samples),
        out_shape=pltpu.VMEM((samples, nt), f32),
        in_specs=[any_spec] * 8,
        out_specs=vmem,
        scratch_shapes=[
            pltpu.VMEM((samples, SEQ, width), bf16),
            pltpu.VMEM((samples, SEQ, width), bf16),
            pltpu.VMEM((rank, width), bf16),
            pltpu.VMEM((width, rank), bf16),
            pltpu.VMEM((2, width, KP), bf16),
            pltpu.VMEM((samples, 1, SEQ), jnp.int32),
            pltpu.VMEM((2, KQ, rank), bf16),
            pltpu.VMEM((nt, KQ * KQ), f32),
            pltpu.VMEM((2, KP + 2 * KQ, width), bf16),
            pltpu.VMEM((samples, 2, KP, SEQ), bf16),
            pltpu.VMEM((samples, 2, KP, SEQ), bf16),
            pltpu.VMEM((samples, 2 * KQ, SEQ), f32),
            pltpu.VMEM((samples, 2 * KQ, SEQ), f32),
            pltpu.VMEM((KQ * KQ, 2 * nt), f32),
            pltpu.VMEM((KQ, KQ * nt), f32),
            pltpu.VMEM((8, KQ, KQ * nt), f32),
            pltpu.VMEM((16 * KQ, KQ * nt), bf16),
            pltpu.VMEM((8 * KQ, KQ * nt), bf16),
            pltpu.VMEM((samples, 2, 2, KQ, 128), f32),
            pltpu.VMEM((4, samples, KQ, 128), f32),
            pltpu.VMEM((2, samples * KQ, 128), f32),
            pltpu.VMEM((2, samples + 8, 2 * nt), f32),
            pltpu.VMEM((4, samples + 8, 2 * nt), f32),
            dma((samples,)), dma((samples,)), dma((7,)),
            dma((11,)), dma((8,)),
            dma((samples,)), dma((samples,)),
            dma((3, samples)), dma((4, samples)),
            dma((3,)), dma((4,)),
        ],
        compiler_params=pltpu.CompilerParams(
            collective_id=0, has_side_effects=True, vmem_limit_bytes=60 << 20
        ),
        name="influence",
    )(inputs, cotangents, loss_token_mask.reshape(samples, 1, SEQ), adapter_down_weight,
      adapter_up_weight, width_projection, jnp.swapaxes(rank_projection, 1, 2), targets)


def general(inputs, cotangents, loss_token_mask, adapter_down_weight, adapter_up_weight,
            width_projection, rank_projection, targets):
    samples = inputs.shape[0] // SEQ
    masked_gradient = cotangents * loss_token_mask.astype(bf16)[:, None]
    cols_first = rank_projection[0].astype(f32)
    cols_second = rank_projection[1].astype(f32)
    down_partial = jnp.dot(inputs, adapter_down_weight.T, preferred_element_type=f32)
    up_partial = jnp.dot(masked_gradient, adapter_up_weight, preferred_element_type=f32)
    exact = lax.Precision.HIGHEST
    compact_up, compact_down = lax.psum(
        (jnp.dot(up_partial, cols_first, precision=exact), jnp.dot(down_partial, cols_second, precision=exact)), "mp"
    )
    projected_x = jnp.dot(inputs, width_projection[0], preferred_element_type=f32).reshape(samples, SEQ, KP)
    projected_g = jnp.dot(masked_gradient, width_projection[1], preferred_element_type=f32).reshape(samples, SEQ, KP)
    first = adapter_scale * jnp.einsum(
        "stk,stq->skq", projected_x, compact_up.reshape(samples, SEQ, KQ), precision=exact)
    second = adapter_scale * jnp.einsum(
        "stk,stq->skq", projected_g, compact_down.reshape(samples, SEQ, KQ), precision=exact)
    partial_value = jnp.concatenate([first.reshape(samples, -1), second.reshape(samples, -1)], axis=1)
    features = lax.psum(partial_value, "mp")
    every_target = lax.all_gather(targets, ("dp", "mp"), axis=1, tiled=True)
    inner = jnp.dot(features, every_target.T, precision=exact)
    sample_rms = jnp.sqrt(jnp.sum(features * features, axis=1) / FEAT + epsilon)
    target_rms = jnp.sqrt(jnp.sum(every_target * every_target, axis=1) / FEAT + epsilon)
    return inner / (math.sqrt(FEAT) * sample_rms[:, None] * target_rms[None, :])


def solution(mesh):
    n_dp, n_mp = mesh.shape["dp"], mesh.shape["mp"]
    fits = n_mp == 2 and n_dp * n_mp * KQ * KQ == FEAT

    def on_device(*args):
        eight = args[0].shape[0] == 8 * SEQ
        return fused(*args) if fits and eight else general(*args)

    in_specs = (
        P("dp", "mp"), P("dp", "mp"), P("dp"), P(None, "mp"), P("mp", None), P(None, "mp", None), P(),
        P(None, ("dp", "mp")),
    )
    return jax.shard_map(on_device, mesh=mesh, in_specs=in_specs, out_specs=P("dp", None), check_vma=False)
```

```python
import functools
import math

import jax
import jax.numpy as jnp
from jax import lax
from jax.experimental import pallas as pl
from jax.experimental.pallas import tpu as pltpu
from jax.sharding import PartitionSpec as P

SEQ = 256
KP = 256
KQ = 16
FEAT = 8192
LAG = 2
PASS = 6
EARLY = 0
NEAR = 3

adapter_scale = 4.0
epsilon = 1e-06

f32 = jnp.float32
bf16 = jnp.bfloat16
NT = (((1,), (1,)), ((), ()))


def split(value):
    high = value.astype(bf16)
    low = (value - high.astype(f32)).astype(bf16)
    return high, low


def kernel(
    samples,
    x_hbm, g_hbm, mask_hbm, down_hbm, up_hbm, wp_hbm, rp_hbm, tgt_hbm, out_ref,
    xv, gv, dv, uv, wv, mv, rv, tv, lhs, ph, pw, cs, cr, tp, tt, ts, th, tl, fs, fr, ft, es, er,
    xsem, gsem, wsem, tsend, trecv, csend, crecv, fsend, frecv, esend, erecv,
):
    me = lax.axis_index("dp")
    core = lax.axis_index("mp")
    z = lax.div(me, 4)
    mine_p = lax.rem(me, 4)
    y = lax.div(mine_p, 2)
    x = lax.rem(mine_p, 2)
    matrix = lax.div(z, 2)
    plane = lax.rem(z, 2)
    slot = plane * 4 + y * 2 + core
    partner = me + 1 - 2 * x
    beyond = me + 8 - 16 * matrix
    holder = core == matrix
    nt = tv.shape[0]
    mesh_ids = pl.DeviceIdType.MESH

    tgt_copy = pltpu.make_async_copy(tgt_hbm, tv, wsem.at[0])
    rp_copy = pltpu.make_async_copy(rp_hbm, rv, wsem.at[1])
    down_copy = pltpu.make_async_copy(down_hbm, dv, wsem.at[2])
    up_copy = pltpu.make_async_copy(up_hbm, uv, wsem.at[3])
    mask_copy = pltpu.make_async_copy(mask_hbm, mv, wsem.at[4])

    def wp_copy(j):
        return pltpu.make_async_copy(wp_hbm.at[j], wv.at[j], wsem.at[5 + j])

    def x_copy(n):
        rows = pl.ds(pl.multiple_of(n * SEQ, SEQ), SEQ)
        return pltpu.make_async_copy(x_hbm.at[rows], xv.at[n], xsem.at[n])

    def g_copy(n):
        rows = pl.ds(pl.multiple_of(n * SEQ, SEQ), SEQ)
        return pltpu.make_async_copy(g_hbm.at[rows], gv.at[n], gsem.at[n])

    tgt_copy.start()
    rp_copy.start()
    down_copy.start()
    up_copy.start()
    mask_copy.start()
    for j in range(2):
        wp_copy(j).start()
    for n in range(samples):
        x_copy(n).start(priority=1)
        g_copy(n).start(priority=1)

    peer = {"dp": me, "mp": 1 - core}

    def close(m):
        there = me
        if m % 2:
            there = there + 2 - 4 * y
        if m // 2:
            there = there + 4 - 8 * plane
        return there

    barrier = pltpu.get_barrier_semaphore()

    def greet(device):
        pl.semaphore_signal(barrier, inc=1, device_id=device, device_id_type=mesh_ids)

    greet(peer)
    for c in range(2):
        greet({"dp": partner, "mp": c})
    for m in range(1, 4):
        greet({"dp": close(m), "mp": core})

    @pl.when(holder)
    def _():
        for m in range(1, 4):
            greet({"dp": close(m), "mp": 1 - core})

    @pl.when(jnp.logical_not(holder))
    def _():
        for c in range(2):
            greet({"dp": beyond, "mp": c})

    tgt_copy.wait()
    turned = tv[...].T
    tp[:, 0:nt] = turned
    tp[:, nt : 2 * nt] = turned
    lane = lax.broadcasted_iota(jnp.int32, (KQ, 2 * nt), 1)
    for pair in range(KQ // 2):
        even = tp[pl.ds(2 * pair, KQ, stride=KQ), :]
        odd = tp[pl.ds(2 * pair + 1, KQ, stride=KQ), :]
        tt[:, pair * 2 * nt : (pair + 1) * 2 * nt] = jnp.where(lane < nt, even, odd)

    rp_copy.wait()
    down_copy.wait()
    first = jnp.dot(rv[1], dv[...], preferred_element_type=f32)
    high, low = split(first)
    lhs[0, KP : KP + KQ] = high
    lhs[0, KP + KQ : KP + 2 * KQ] = low
    up_copy.wait()
    second = lax.dot_general(rv[0], uv[...], NT, preferred_element_type=f32)
    high, low = split(second)
    lhs[1, KP : KP + KQ] = high
    lhs[1, KP + KQ : KP + 2 * KQ] = low
    for j in range(2):
        wp_copy(j).wait()
        flat = wv[j].T
        for p in range(8):
            start = p % 2 * 128 + p // 2 * 32
            lhs[j, start : start + 32] = flat[p * 32 : (p + 1) * 32]

    def t_copy(way):
        if way < 3:
            there = {"dp": close(way + 1), "mp": matrix}
        elif way == 3:
            there = {"dp": beyond, "mp": matrix}
        else:
            there = peer
        return pltpu.make_async_remote_copy(
            src_ref=tt, dst_ref=ts.at[slot], send_sem=tsend.at[way], recv_sem=trecv.at[slot],
            device_id=there, device_id_type=mesh_ids,
        )

    def t_pass(c, m):
        held = plane * 4 + y * 2 + c
        return pltpu.make_async_remote_copy(
            src_ref=ts.at[held], dst_ref=ts.at[held], send_sem=tsend.at[4 + c * 3 + m], recv_sem=trecv.at[held],
            device_id={"dp": close(m), "mp": core}, device_id_type=mesh_ids,
        )

    def t_arrival(i):
        return pltpu.make_async_remote_copy(
            src_ref=tt, dst_ref=ts.at[i], send_sem=tsend.at[0], recv_sem=trecv.at[i],
            device_id=peer, device_id_type=mesh_ids,
        )

    def c_copy(n):
        return pltpu.make_async_remote_copy(
            src_ref=cs.at[n], dst_ref=cr.at[n], send_sem=csend.at[n], recv_sem=crecv.at[n],
            device_id=peer, device_id_type=mesh_ids,
        )

    def f_near(n):
        return pltpu.make_async_remote_copy(
            src_ref=fs.at[n, 1 - core, x], dst_ref=fr.at[core, n],
            send_sem=fsend.at[2, n], recv_sem=frecv.at[core, n],
            device_id=peer, device_id_type=mesh_ids,
        )

    def f_far(n, h):
        return pltpu.make_async_remote_copy(
            src_ref=fs.at[n, h, 1 - x], dst_ref=fr.at[2 + core, n],
            send_sem=fsend.at[h, n], recv_sem=frecv.at[2 + core, n],
            device_id={"dp": partner, "mp": h}, device_id_type=mesh_ids,
        )

    def f_arrival(source, n):
        return pltpu.make_async_remote_copy(
            src_ref=fs.at[n, 0, 0], dst_ref=fr.at[source, n],
            send_sem=fsend.at[0, n], recv_sem=frecv.at[source, n],
            device_id=peer, device_id_type=mesh_ids,
        )

    def phase_one(n):
        for j, data in enumerate((xv, gv)):
            out = lax.dot_general(lhs[j], data[n], NT, preferred_element_type=f32)
            high, low = split(out[0:KP])
            ph[n, j] = high
            pw[n, j] = low
            cs[n, j * KQ : (j + 1) * KQ] = out[KP : KP + KQ] + out[KP + KQ : KP + 2 * KQ]

    def phase_two(n):
        flags = mv[n].astype(f32) * adapter_scale
        total = (cs[n] + cr[n]) * flags
        for j in range(2):
            high, low = split(total[(1 - j) * KQ : (2 - j) * KQ])
            stacked = jnp.concatenate([high, low], axis=0)
            out = lax.dot_general(stacked, ph[n, j], NT, preferred_element_type=f32)
            rest = lax.dot_general(high, pw[n, j], NT, preferred_element_type=f32)
            feature = out[0:KQ] + out[KQ : 2 * KQ] + rest
            for h in range(2):
                fs[n, j, h] = feature[:, h * 128 : (h + 1) * 128]

    def fetch(n):
        x_copy(n).wait()
        g_copy(n).wait()

    def send_features(n):
        for h in range(2):
            f_far(n, h).start()
        f_near(n).start()

    def only_one(n, carry):
        fetch(n)
        phase_one(n)
        return carry

    def both(n, carry):
        fetch(n)
        c_copy(n - LAG).wait_recv()
        phase_one(n)
        phase_two(n - LAG)
        c_copy(n).start()
        send_features(n - LAG)
        return carry

    def catch_up(n):
        fetch(n)
        for old in range(n - LAG - 1, n - LAG + 1):
            c_copy(old).wait_recv()
        phase_one(n)
        for old in range(n - LAG - 1, n - LAG + 1):
            phase_two(old)
        c_copy(n).start()
        for old in range(n - LAG - 1, n - LAG + 1):
            send_features(old)

    def only_two(n, carry):
        c_copy(n).wait_recv()
        phase_two(n)
        send_features(n)
        return carry

    def start_c(n, carry):
        c_copy(n).start()
        return carry

    lax.fori_loop(0, EARLY, only_one, 0)
    pl.semaphore_wait(barrier, jnp.where(holder, 7, 10))
    lax.fori_loop(0, EARLY, start_c, 0)
    t_copy(3).start()

    @pl.when(jnp.logical_not(holder))
    def _():
        t_copy(4).start()

    @pl.when(holder)
    def _():
        ts[slot] = tt[...]

    def one_more(n, carry):
        only_one(n, carry)
        c_copy(n).start()
        return carry

    lax.fori_loop(EARLY, LAG + 1, one_more, 0)
    mask_copy.wait()
    for way in range(3):
        t_copy(way).start()
    catch_up(LAG + 1)
    lax.fori_loop(LAG + 2, PASS, both, 0)

    @pl.when(jnp.logical_not(holder))
    def _():
        for c in range(2):
            t_arrival(plane * 4 + y * 2 + c).wait_recv()
            for m in range(1, 4):
                t_pass(c, m).start()

    lax.fori_loop(PASS, samples, both, 0)
    lax.fori_loop(samples - LAG, samples, only_two, 0)

    def take(line):
        total = None
        for p in range(2):
            start = pl.multiple_of(p * 4 + line * 2, 2)
            held = ts[pl.ds(start, 2)].reshape(2 * KQ, KQ * nt)
            t_high, t_low = split(held)
            row = pl.multiple_of(start * KQ, 2 * KQ)
            th[pl.ds(row, 2 * KQ)] = t_high
            th[pl.ds(row + 8 * KQ, 2 * KQ)] = t_high
            tl[pl.ds(row, 2 * KQ)] = t_low
            part = jnp.sum((held * held).reshape(4, 8, KQ * nt), axis=0)
            total = part if total is None else total + part
        folded = total[:, 0 : 2 * nt]
        for piece in range(1, KQ // 2):
            folded = folded + total[:, piece * 2 * nt : (piece + 1) * 2 * nt]
        return folded

    @pl.when(holder)
    def _():
        t_arrival(plane * 4 + y * 2 + 1 - core).wait_recv()

    for m in range(1, 4):
        row = y + (1 - 2 * y) * (m % 2)
        side = plane + (1 - 2 * plane) * (m // 2)
        for c in range(2):
            t_arrival(side * 4 + row * 2 + c).wait_recv()
    folded = take(0) + take(1)
    left_lane = lax.broadcasted_iota(jnp.int32, (samples, 2 * nt), 1) < nt

    def score(side):
        if side == 0:
            total = fr[1 - core] + fs[:, core, x]
        else:
            total = fr[2] + fr[3]
        ft[side] = total.reshape(samples * KQ, 128)
        power = None
        even = None
        odd = None
        for step in range(4):
            rows = [ft[side, pl.ds(4 * step + r, samples, stride=KQ), :] for r in range(4)]
            for row in rows:
                power = row * row if power is None else power + row * row
            high, low = split(jnp.concatenate(rows, axis=0))
            cols = slice(step * 4 * nt, (step + 1) * 4 * nt)
            out = jnp.dot(jnp.concatenate([high, low], axis=1), th[:, cols], preferred_element_type=f32)
            out = out + jnp.dot(high, tl[:, cols], preferred_element_type=f32)
            first = out[0:samples, 0 : 2 * nt] + out[2 * samples : 3 * samples, 2 * nt : 4 * nt]
            second = out[samples : 2 * samples, 0 : 2 * nt] + out[3 * samples : 4 * samples, 2 * nt : 4 * nt]
            even = first if even is None else even + first
            odd = second if odd is None else odd + second
        inner = jnp.where(left_lane, even, odd)
        inner = inner + pltpu.roll(inner, nt, 1)
        power = power + pltpu.roll(power, nt, 1)
        es[side, 0:samples] = jnp.where(left_lane, inner, power)
        es[side, samples : samples + 8] = folded

    def e_near():
        return pltpu.make_async_remote_copy(
            src_ref=es.at[0], dst_ref=er.at[core], send_sem=esend.at[2], recv_sem=erecv.at[core],
            device_id=peer, device_id_type=mesh_ids,
        )

    def e_far(h):
        return pltpu.make_async_remote_copy(
            src_ref=es.at[1], dst_ref=er.at[2 + core], send_sem=esend.at[h], recv_sem=erecv.at[2 + core],
            device_id={"dp": partner, "mp": h}, device_id_type=mesh_ids,
        )

    def e_arrival(source):
        return pltpu.make_async_remote_copy(
            src_ref=es.at[0], dst_ref=er.at[source], send_sem=esend.at[0], recv_sem=erecv.at[source],
            device_id=peer, device_id_type=mesh_ids,
        )

    def near_arrived(n, carry):
        f_arrival(1 - core, n).wait_recv()
        return carry

    def far_arrived(n, carry):
        f_arrival(2, n).wait_recv()
        f_arrival(3, n).wait_recv()
        return carry

    def all_sent(n, carry):
        c_copy(n).wait_send()
        f_near(n).wait_send()
        for h in range(2):
            f_far(n, h).wait_send()
        return carry

    lax.fori_loop(0, samples, near_arrived, 0)
    score(0)
    e_near().start()
    er[core] = es[0]
    lax.fori_loop(0, samples, far_arrived, 0)
    score(1)
    for h in range(2):
        e_far(h).start()
    lax.fori_loop(0, samples, all_sent, 0)
    for way in range(4):
        t_copy(way).wait_send()

    @pl.when(jnp.logical_not(holder))
    def _():
        t_copy(4).wait_send()

    @pl.when(jnp.logical_not(holder))
    def _():
        for c in range(2):
            for m in range(1, 4):
                t_pass(c, m).wait_send()

    e_arrival(1 - core).wait_recv()
    for source in (2, 3):
        e_arrival(source).wait_recv()
    total = er[0] + er[1] + er[2] + er[3]
    target_squares = jnp.sum(total[samples : samples + 8], axis=0, keepdims=True)
    target_squares = target_squares[:, 0:nt] + target_squares[:, nt : 2 * nt]
    target_rms = jnp.sqrt(target_squares / FEAT + epsilon)
    sample_squares = jnp.sum(total[0:samples, nt : 2 * nt], axis=1, keepdims=True)
    sample_rms = jnp.sqrt(sample_squares / FEAT + epsilon)
    out_ref[...] = total[0:samples, 0:nt] / (math.sqrt(FEAT) * sample_rms * target_rms)
    e_near().wait_send()
    for h in range(2):
        e_far(h).wait_send()


def fused(inputs, cotangents, loss_token_mask, adapter_down_weight, adapter_up_weight,
          width_projection, rank_projection, targets):
    samples = inputs.shape[0] // SEQ
    width = inputs.shape[1]
    rank = adapter_down_weight.shape[0]
    nt = targets.shape[0]
    any_spec = pl.BlockSpec(memory_space=pltpu.HBM)
    vmem = pl.BlockSpec(memory_space=pltpu.VMEM)
    dma = pltpu.SemaphoreType.DMA
    return pl.pallas_call(
        functools.partial(kernel, samples),
        out_shape=pltpu.VMEM((samples, nt), f32),
        in_specs=[any_spec] * 8,
        out_specs=vmem,
        scratch_shapes=[
            pltpu.VMEM((samples, SEQ, width), bf16),
            pltpu.VMEM((samples, SEQ, width), bf16),
            pltpu.VMEM((rank, width), bf16),
            pltpu.VMEM((width, rank), bf16),
            pltpu.VMEM((2, width, KP), bf16),
            pltpu.VMEM((samples, 1, SEQ), jnp.int32),
            pltpu.VMEM((2, KQ, rank), bf16),
            pltpu.VMEM((nt, KQ * KQ), f32),
            pltpu.VMEM((2, KP + 2 * KQ, width), bf16),
            pltpu.VMEM((samples, 2, KP, SEQ), bf16),
            pltpu.VMEM((samples, 2, KP, SEQ), bf16),
            pltpu.VMEM((samples, 2 * KQ, SEQ), f32),
            pltpu.VMEM((samples, 2 * KQ, SEQ), f32),
            pltpu.VMEM((KQ * KQ, 2 * nt), f32),
            pltpu.VMEM((KQ, KQ * nt), f32),
            pltpu.VMEM((8, KQ, KQ * nt), f32),
            pltpu.VMEM((16 * KQ, KQ * nt), bf16),
            pltpu.VMEM((8 * KQ, KQ * nt), bf16),
            pltpu.VMEM((samples, 2, 2, KQ, 128), f32),
            pltpu.VMEM((4, samples, KQ, 128), f32),
            pltpu.VMEM((2, samples * KQ, 128), f32),
            pltpu.VMEM((2, samples + 8, 2 * nt), f32),
            pltpu.VMEM((4, samples + 8, 2 * nt), f32),
            dma((samples,)), dma((samples,)), dma((7,)),
            dma((11,)), dma((8,)),
            dma((samples,)), dma((samples,)),
            dma((3, samples)), dma((4, samples)),
            dma((3,)), dma((4,)),
        ],
        compiler_params=pltpu.CompilerParams(
            collective_id=0, has_side_effects=True, vmem_limit_bytes=60 << 20
        ),
        name="influence",
    )(inputs, cotangents, loss_token_mask.reshape(samples, 1, SEQ), adapter_down_weight,
      adapter_up_weight, width_projection, jnp.swapaxes(rank_projection, 1, 2), targets)


def general(inputs, cotangents, loss_token_mask, adapter_down_weight, adapter_up_weight,
            width_projection, rank_projection, targets):
    samples = inputs.shape[0] // SEQ
    masked_gradient = cotangents * loss_token_mask.astype(bf16)[:, None]
    cols_first = rank_projection[0].astype(f32)
    cols_second = rank_projection[1].astype(f32)
    down_partial = jnp.dot(inputs, adapter_down_weight.T, preferred_element_type=f32)
    up_partial = jnp.dot(masked_gradient, adapter_up_weight, preferred_element_type=f32)
    exact = lax.Precision.HIGHEST
    compact_up, compact_down = lax.psum(
        (jnp.dot(up_partial, cols_first, precision=exact), jnp.dot(down_partial, cols_second, precision=exact)), "mp"
    )
    projected_x = jnp.dot(inputs, width_projection[0], preferred_element_type=f32).reshape(samples, SEQ, KP)
    projected_g = jnp.dot(masked_gradient, width_projection[1], preferred_element_type=f32).reshape(samples, SEQ, KP)
    first = adapter_scale * jnp.einsum(
        "stk,stq->skq", projected_x, compact_up.reshape(samples, SEQ, KQ), precision=exact)
    second = adapter_scale * jnp.einsum(
        "stk,stq->skq", projected_g, compact_down.reshape(samples, SEQ, KQ), precision=exact)
    partial_value = jnp.concatenate([first.reshape(samples, -1), second.reshape(samples, -1)], axis=1)
    features = lax.psum(partial_value, "mp")
    every_target = lax.all_gather(targets, ("dp", "mp"), axis=1, tiled=True)
    inner = jnp.dot(features, every_target.T, precision=exact)
    sample_rms = jnp.sqrt(jnp.sum(features * features, axis=1) / FEAT + epsilon)
    target_rms = jnp.sqrt(jnp.sum(every_target * every_target, axis=1) / FEAT + epsilon)
    return inner / (math.sqrt(FEAT) * sample_rms[:, None] * target_rms[None, :])


def solution(mesh):
    n_dp, n_mp = mesh.shape["dp"], mesh.shape["mp"]
    fits = n_mp == 2 and n_dp * n_mp * KQ * KQ == FEAT

    def on_device(*args):
        eight = args[0].shape[0] == 8 * SEQ
        return fused(*args) if fits and eight else general(*args)

    in_specs = (
        P("dp", "mp"), P("dp", "mp"), P("dp"), P(None, "mp"), P("mp", None), P(None, "mp", None), P(),
        P(None, ("dp", "mp")),
    )
    return jax.shard_map(on_device, mesh=mesh, in_specs=in_specs, out_specs=P("dp", None), check_vma=False)
```

```python
import functools
import math

import jax
import jax.numpy as jnp
from jax import lax
from jax.experimental import pallas as pl
from jax.experimental.pallas import tpu as pltpu
from jax.sharding import PartitionSpec as P

SEQ = 256
KP = 256
KQ = 16
FEAT = 8192
LAG = 2
PASS = 6
EARLY = 0
NEAR = 3

adapter_scale = 4.0
epsilon = 1e-06

f32 = jnp.float32
bf16 = jnp.bfloat16
NT = (((1,), (1,)), ((), ()))


def split(value):
    high = value.astype(bf16)
    low = (value - high.astype(f32)).astype(bf16)
    return high, low


def kernel(
    samples,
    x_hbm, g_hbm, mask_hbm, down_hbm, up_hbm, wp_hbm, rp_hbm, tgt_hbm, out_ref,
    xv, gv, dv, uv, wv, mv, rv, tv, lhs, ph, pw, cs, cr, tp, tt, ts, th, tl, fs, fr, ft, es, er,
    xsem, gsem, wsem, tsend, trecv, csend, crecv, fsend, frecv, esend, erecv,
):
    me = lax.axis_index("dp")
    core = lax.axis_index("mp")
    z = lax.div(me, 4)
    mine_p = lax.rem(me, 4)
    y = lax.div(mine_p, 2)
    x = lax.rem(mine_p, 2)
    matrix = lax.div(z, 2)
    plane = lax.rem(z, 2)
    slot = plane * 4 + y * 2 + core
    partner = me + 1 - 2 * x
    beyond = me + 8 - 16 * matrix
    holder = core == matrix
    nt = tv.shape[0]
    mesh_ids = pl.DeviceIdType.MESH

    tgt_copy = pltpu.make_async_copy(tgt_hbm, tv, wsem.at[0])
    rp_copy = pltpu.make_async_copy(rp_hbm, rv, wsem.at[1])
    down_copy = pltpu.make_async_copy(down_hbm, dv, wsem.at[2])
    up_copy = pltpu.make_async_copy(up_hbm, uv, wsem.at[3])
    mask_copy = pltpu.make_async_copy(mask_hbm, mv, wsem.at[4])

    def wp_copy(j):
        return pltpu.make_async_copy(wp_hbm.at[j], wv.at[j], wsem.at[5 + j])

    def x_copy(n):
        rows = pl.ds(pl.multiple_of(n * SEQ, SEQ), SEQ)
        return pltpu.make_async_copy(x_hbm.at[rows], xv.at[n], xsem.at[n])

    def g_copy(n):
        rows = pl.ds(pl.multiple_of(n * SEQ, SEQ), SEQ)
        return pltpu.make_async_copy(g_hbm.at[rows], gv.at[n], gsem.at[n])

    tgt_copy.start()
    rp_copy.start()
    down_copy.start()
    up_copy.start()
    mask_copy.start()
    for j in range(2):
        wp_copy(j).start()
    for n in range(samples):
        x_copy(n).start(priority=1)
        g_copy(n).start(priority=1)

    peer = {"dp": me, "mp": 1 - core}

    def close(m):
        there = me
        if m % 2:
            there = there + 2 - 4 * y
        if m // 2:
            there = there + 4 - 8 * plane
        return there

    barrier = pltpu.get_barrier_semaphore()

    def greet(device):
        pl.semaphore_signal(barrier, inc=1, device_id=device, device_id_type=mesh_ids)

    greet(peer)
    for c in range(2):
        greet({"dp": partner, "mp": c})
    for m in range(1, 4):
        greet({"dp": close(m), "mp": core})

    @pl.when(holder)
    def _():
        for m in range(1, 4):
            greet({"dp": close(m), "mp": 1 - core})

    @pl.when(jnp.logical_not(holder))
    def _():
        for c in range(2):
            greet({"dp": beyond, "mp": c})

    tgt_copy.wait()
    turned = tv[...].T
    tp[:, 0:nt] = turned
    tp[:, nt : 2 * nt] = turned
    lane = lax.broadcasted_iota(jnp.int32, (KQ, 2 * nt), 1)
    for pair in range(KQ // 2):
        even = tp[pl.ds(2 * pair, KQ, stride=KQ), :]
        odd = tp[pl.ds(2 * pair + 1, KQ, stride=KQ), :]
        tt[:, pair * 2 * nt : (pair + 1) * 2 * nt] = jnp.where(lane < nt, even, odd)

    rp_copy.wait()
    down_copy.wait()
    first = jnp.dot(rv[1], dv[...], preferred_element_type=f32)
    high, low = split(first)
    lhs[0, KP : KP + KQ] = high
    lhs[0, KP + KQ : KP + 2 * KQ] = low
    up_copy.wait()
    second = lax.dot_general(rv[0], uv[...], NT, preferred_element_type=f32)
    high, low = split(second)
    lhs[1, KP : KP + KQ] = high
    lhs[1, KP + KQ : KP + 2 * KQ] = low
    for j in range(2):
        wp_copy(j).wait()
        flat = wv[j].T
        for p in range(8):
            start = p % 2 * 128 + p // 2 * 32
            lhs[j, start : start + 32] = flat[p * 32 : (p + 1) * 32]

    def t_copy(way):
        if way < 3:
            there = {"dp": close(way + 1), "mp": matrix}
        elif way == 3:
            there = {"dp": beyond, "mp": matrix}
        else:
            there = peer
        return pltpu.make_async_remote_copy(
            src_ref=tt, dst_ref=ts.at[slot], send_sem=tsend.at[way], recv_sem=trecv.at[slot],
            device_id=there, device_id_type=mesh_ids,
        )

    def t_pass(c, m):
        held = plane * 4 + y * 2 + c
        return pltpu.make_async_remote_copy(
            src_ref=ts.at[held], dst_ref=ts.at[held], send_sem=tsend.at[4 + c * 3 + m], recv_sem=trecv.at[held],
            device_id={"dp": close(m), "mp": core}, device_id_type=mesh_ids,
        )

    def t_arrival(i):
        return pltpu.make_async_remote_copy(
            src_ref=tt, dst_ref=ts.at[i], send_sem=tsend.at[0], recv_sem=trecv.at[i],
            device_id=peer, device_id_type=mesh_ids,
        )

    def c_copy(n):
        return pltpu.make_async_remote_copy(
            src_ref=cs.at[n], dst_ref=cr.at[n], send_sem=csend.at[n], recv_sem=crecv.at[n],
            device_id=peer, device_id_type=mesh_ids,
        )

    def f_near(n):
        return pltpu.make_async_remote_copy(
            src_ref=fs.at[n, 1 - core, x], dst_ref=fr.at[core, n],
            send_sem=fsend.at[2, n], recv_sem=frecv.at[core, n],
            device_id=peer, device_id_type=mesh_ids,
        )

    def f_far(n, h):
        return pltpu.make_async_remote_copy(
            src_ref=fs.at[n, h, 1 - x], dst_ref=fr.at[2 + core, n],
            send_sem=fsend.at[h, n], recv_sem=frecv.at[2 + core, n],
            device_id={"dp": partner, "mp": h}, device_id_type=mesh_ids,
        )

    def f_arrival(source, n):
        return pltpu.make_async_remote_copy(
            src_ref=fs.at[n, 0, 0], dst_ref=fr.at[source, n],
            send_sem=fsend.at[0, n], recv_sem=frecv.at[source, n],
            device_id=peer, device_id_type=mesh_ids,
        )

    def phase_one(n):
        for j, data in enumerate((xv, gv)):
            out = lax.dot_general(lhs[j], data[n], NT, preferred_element_type=f32)
            high, low = split(out[0:KP])
            ph[n, j] = high
            pw[n, j] = low
            cs[n, j * KQ : (j + 1) * KQ] = out[KP : KP + KQ] + out[KP + KQ : KP + 2 * KQ]

    def phase_two(n):
        flags = mv[n].astype(f32) * adapter_scale
        total = (cs[n] + cr[n]) * flags
        for j in range(2):
            high, low = split(total[(1 - j) * KQ : (2 - j) * KQ])
            stacked = jnp.concatenate([high, low], axis=0)
            out = lax.dot_general(stacked, ph[n, j], NT, preferred_element_type=f32)
            rest = lax.dot_general(high, pw[n, j], NT, preferred_element_type=f32)
            feature = out[0:KQ] + out[KQ : 2 * KQ] + rest
            for h in range(2):
                fs[n, j, h] = feature[:, h * 128 : (h + 1) * 128]

    def fetch(n):
        x_copy(n).wait()
        g_copy(n).wait()

    def send_features(n):
        for h in range(2):
            f_far(n, h).start()
        f_near(n).start()

    def only_one(n, carry):
        fetch(n)
        phase_one(n)
        return carry

    def both(n, carry):
        fetch(n)
        c_copy(n - LAG).wait_recv()
        phase_one(n)
        phase_two(n - LAG)
        c_copy(n).start()
        send_features(n - LAG)
        return carry

    def catch_up(n):
        fetch(n)
        for old in range(n - LAG - 1, n - LAG + 1):
            c_copy(old).wait_recv()
        phase_one(n)
        for old in range(n - LAG - 1, n - LAG + 1):
            phase_two(old)
        c_copy(n).start()
        for old in range(n - LAG - 1, n - LAG + 1):
            send_features(old)

    def only_two(n, carry):
        c_copy(n).wait_recv()
        phase_two(n)
        send_features(n)
        return carry

    def start_c(n, carry):
        c_copy(n).start()
        return carry

    lax.fori_loop(0, EARLY, only_one, 0)
    pl.semaphore_wait(barrier, jnp.where(holder, 7, 10))
    lax.fori_loop(0, EARLY, start_c, 0)
    t_copy(3).start()

    @pl.when(jnp.logical_not(holder))
    def _():
        t_copy(4).start()

    @pl.when(holder)
    def _():
        ts[slot] = tt[...]

    def one_more(n, carry):
        only_one(n, carry)
        c_copy(n).start()
        return carry

    lax.fori_loop(EARLY, LAG + 1, one_more, 0)
    mask_copy.wait()
    for way in range(3):
        t_copy(way).start()
    catch_up(LAG + 1)
    lax.fori_loop(LAG + 2, PASS, both, 0)

    @pl.when(jnp.logical_not(holder))
    def _():
        for c in range(2):
            t_arrival(plane * 4 + y * 2 + c).wait_recv()
            for m in (3, 1, 2):
                t_pass(c, m).start()

    lax.fori_loop(PASS, samples, both, 0)
    lax.fori_loop(samples - LAG, samples, only_two, 0)

    def take(line):
        total = None
        for p in range(2):
            start = pl.multiple_of(p * 4 + line * 2, 2)
            held = ts[pl.ds(start, 2)].reshape(2 * KQ, KQ * nt)
            t_high, t_low = split(held)
            row = pl.multiple_of(start * KQ, 2 * KQ)
            th[pl.ds(row, 2 * KQ)] = t_high
            th[pl.ds(row + 8 * KQ, 2 * KQ)] = t_high
            tl[pl.ds(row, 2 * KQ)] = t_low
            part = jnp.sum((held * held).reshape(4, 8, KQ * nt), axis=0)
            total = part if total is None else total + part
        folded = total[:, 0 : 2 * nt]
        for piece in range(1, KQ // 2):
            folded = folded + total[:, piece * 2 * nt : (piece + 1) * 2 * nt]
        return folded

    @pl.when(holder)
    def _():
        t_arrival(plane * 4 + y * 2 + 1 - core).wait_recv()

    for m in range(1, 4):
        row = y + (1 - 2 * y) * (m % 2)
        side = plane + (1 - 2 * plane) * (m // 2)
        for c in range(2):
            t_arrival(side * 4 + row * 2 + c).wait_recv()
    folded = take(0) + take(1)
    left_lane = lax.broadcasted_iota(jnp.int32, (samples, 2 * nt), 1) < nt

    def score(side):
        if side == 0:
            total = fr[1 - core] + fs[:, core, x]
        else:
            total = fr[2] + fr[3]
        ft[side] = total.reshape(samples * KQ, 128)
        power = None
        even = None
        odd = None
        for step in range(4):
            rows = [ft[side, pl.ds(4 * step + r, samples, stride=KQ), :] for r in range(4)]
            for row in rows:
                power = row * row if power is None else power + row * row
            high, low = split(jnp.concatenate(rows, axis=0))
            cols = slice(step * 4 * nt, (step + 1) * 4 * nt)
            out = jnp.dot(jnp.concatenate([high, low], axis=1), th[:, cols], preferred_element_type=f32)
            out = out + jnp.dot(high, tl[:, cols], preferred_element_type=f32)
            first = out[0:samples, 0 : 2 * nt] + out[2 * samples : 3 * samples, 2 * nt : 4 * nt]
            second = out[samples : 2 * samples, 0 : 2 * nt] + out[3 * samples : 4 * samples, 2 * nt : 4 * nt]
            even = first if even is None else even + first
            odd = second if odd is None else odd + second
        inner = jnp.where(left_lane, even, odd)
        inner = inner + pltpu.roll(inner, nt, 1)
        power = power + pltpu.roll(power, nt, 1)
        es[side, 0:samples] = jnp.where(left_lane, inner, power)
        es[side, samples : samples + 8] = folded

    def e_near():
        return pltpu.make_async_remote_copy(
            src_ref=es.at[0], dst_ref=er.at[core], send_sem=esend.at[2], recv_sem=erecv.at[core],
            device_id=peer, device_id_type=mesh_ids,
        )

    def e_far(h):
        return pltpu.make_async_remote_copy(
            src_ref=es.at[1], dst_ref=er.at[2 + core], send_sem=esend.at[h], recv_sem=erecv.at[2 + core],
            device_id={"dp": partner, "mp": h}, device_id_type=mesh_ids,
        )

    def e_arrival(source):
        return pltpu.make_async_remote_copy(
            src_ref=es.at[0], dst_ref=er.at[source], send_sem=esend.at[0], recv_sem=erecv.at[source],
            device_id=peer, device_id_type=mesh_ids,
        )

    def near_arrived(n, carry):
        f_arrival(1 - core, n).wait_recv()
        return carry

    def far_arrived(n, carry):
        f_arrival(2, n).wait_recv()
        f_arrival(3, n).wait_recv()
        return carry

    def all_sent(n, carry):
        c_copy(n).wait_send()
        f_near(n).wait_send()
        for h in range(2):
            f_far(n, h).wait_send()
        return carry

    lax.fori_loop(0, samples, near_arrived, 0)
    score(0)
    e_near().start()
    er[core] = es[0]
    lax.fori_loop(0, samples, far_arrived, 0)
    score(1)
    for h in range(2):
        e_far(h).start()
    lax.fori_loop(0, samples, all_sent, 0)
    for way in range(4):
        t_copy(way).wait_send()

    @pl.when(jnp.logical_not(holder))
    def _():
        t_copy(4).wait_send()

    @pl.when(jnp.logical_not(holder))
    def _():
        for c in range(2):
            for m in range(1, 4):
                t_pass(c, m).wait_send()

    e_arrival(1 - core).wait_recv()
    for source in (2, 3):
        e_arrival(source).wait_recv()
    total = er[0] + er[1] + er[2] + er[3]
    target_squares = jnp.sum(total[samples : samples + 8], axis=0, keepdims=True)
    target_squares = target_squares[:, 0:nt] + target_squares[:, nt : 2 * nt]
    target_rms = jnp.sqrt(target_squares / FEAT + epsilon)
    sample_squares = jnp.sum(total[0:samples, nt : 2 * nt], axis=1, keepdims=True)
    sample_rms = jnp.sqrt(sample_squares / FEAT + epsilon)
    out_ref[...] = total[0:samples, 0:nt] / (math.sqrt(FEAT) * sample_rms * target_rms)
    e_near().wait_send()
    for h in range(2):
        e_far(h).wait_send()


def fused(inputs, cotangents, loss_token_mask, adapter_down_weight, adapter_up_weight,
          width_projection, rank_projection, targets):
    samples = inputs.shape[0] // SEQ
    width = inputs.shape[1]
    rank = adapter_down_weight.shape[0]
    nt = targets.shape[0]
    any_spec = pl.BlockSpec(memory_space=pltpu.HBM)
    vmem = pl.BlockSpec(memory_space=pltpu.VMEM)
    dma = pltpu.SemaphoreType.DMA
    return pl.pallas_call(
        functools.partial(kernel, samples),
        out_shape=pltpu.VMEM((samples, nt), f32),
        in_specs=[any_spec] * 8,
        out_specs=vmem,
        scratch_shapes=[
            pltpu.VMEM((samples, SEQ, width), bf16),
            pltpu.VMEM((samples, SEQ, width), bf16),
            pltpu.VMEM((rank, width), bf16),
            pltpu.VMEM((width, rank), bf16),
            pltpu.VMEM((2, width, KP), bf16),
            pltpu.VMEM((samples, 1, SEQ), jnp.int32),
            pltpu.VMEM((2, KQ, rank), bf16),
            pltpu.VMEM((nt, KQ * KQ), f32),
            pltpu.VMEM((2, KP + 2 * KQ, width), bf16),
            pltpu.VMEM((samples, 2, KP, SEQ), bf16),
            pltpu.VMEM((samples, 2, KP, SEQ), bf16),
            pltpu.VMEM((samples, 2 * KQ, SEQ), f32),
            pltpu.VMEM((samples, 2 * KQ, SEQ), f32),
            pltpu.VMEM((KQ * KQ, 2 * nt), f32),
            pltpu.VMEM((KQ, KQ * nt), f32),
            pltpu.VMEM((8, KQ, KQ * nt), f32),
            pltpu.VMEM((16 * KQ, KQ * nt), bf16),
            pltpu.VMEM((8 * KQ, KQ * nt), bf16),
            pltpu.VMEM((samples, 2, 2, KQ, 128), f32),
            pltpu.VMEM((4, samples, KQ, 128), f32),
            pltpu.VMEM((2, samples * KQ, 128), f32),
            pltpu.VMEM((2, samples + 8, 2 * nt), f32),
            pltpu.VMEM((4, samples + 8, 2 * nt), f32),
            dma((samples,)), dma((samples,)), dma((7,)),
            dma((11,)), dma((8,)),
            dma((samples,)), dma((samples,)),
            dma((3, samples)), dma((4, samples)),
            dma((3,)), dma((4,)),
        ],
        compiler_params=pltpu.CompilerParams(
            collective_id=0, has_side_effects=True, vmem_limit_bytes=60 << 20
        ),
        name="influence",
    )(inputs, cotangents, loss_token_mask.reshape(samples, 1, SEQ), adapter_down_weight,
      adapter_up_weight, width_projection, jnp.swapaxes(rank_projection, 1, 2), targets)


def general(inputs, cotangents, loss_token_mask, adapter_down_weight, adapter_up_weight,
            width_projection, rank_projection, targets):
    samples = inputs.shape[0] // SEQ
    masked_gradient = cotangents * loss_token_mask.astype(bf16)[:, None]
    cols_first = rank_projection[0].astype(f32)
    cols_second = rank_projection[1].astype(f32)
    down_partial = jnp.dot(inputs, adapter_down_weight.T, preferred_element_type=f32)
    up_partial = jnp.dot(masked_gradient, adapter_up_weight, preferred_element_type=f32)
    exact = lax.Precision.HIGHEST
    compact_up, compact_down = lax.psum(
        (jnp.dot(up_partial, cols_first, precision=exact), jnp.dot(down_partial, cols_second, precision=exact)), "mp"
    )
    projected_x = jnp.dot(inputs, width_projection[0], preferred_element_type=f32).reshape(samples, SEQ, KP)
    projected_g = jnp.dot(masked_gradient, width_projection[1], preferred_element_type=f32).reshape(samples, SEQ, KP)
    first = adapter_scale * jnp.einsum(
        "stk,stq->skq", projected_x, compact_up.reshape(samples, SEQ, KQ), precision=exact)
    second = adapter_scale * jnp.einsum(
        "stk,stq->skq", projected_g, compact_down.reshape(samples, SEQ, KQ), precision=exact)
    partial_value = jnp.concatenate([first.reshape(samples, -1), second.reshape(samples, -1)], axis=1)
    features = lax.psum(partial_value, "mp")
    every_target = lax.all_gather(targets, ("dp", "mp"), axis=1, tiled=True)
    inner = jnp.dot(features, every_target.T, precision=exact)
    sample_rms = jnp.sqrt(jnp.sum(features * features, axis=1) / FEAT + epsilon)
    target_rms = jnp.sqrt(jnp.sum(every_target * every_target, axis=1) / FEAT + epsilon)
    return inner / (math.sqrt(FEAT) * sample_rms[:, None] * target_rms[None, :])


def solution(mesh):
    n_dp, n_mp = mesh.shape["dp"], mesh.shape["mp"]
    fits = n_mp == 2 and n_dp * n_mp * KQ * KQ == FEAT

    def on_device(*args):
        eight = args[0].shape[0] == 8 * SEQ
        return fused(*args) if fits and eight else general(*args)

    in_specs = (
        P("dp", "mp"), P("dp", "mp"), P("dp"), P(None, "mp"), P("mp", None), P(None, "mp", None), P(),
        P(None, ("dp", "mp")),
    )
    return jax.shard_map(on_device, mesh=mesh, in_specs=in_specs, out_specs=P("dp", None), check_vma=False)
```
